256 devices in a mesh: plane: 8 (over z), pencil: 32 (over x, y, core).
Axes of the slice: x: 4, y: 4, z: 8, core: 2. Of those that a mesh axis runs over, the one named last changes fastest.
Arguments:
- velocity: float32 [16, 5120, 3840], P('plane', 'pencil'), may hold values from -6 to 6
- plane_slot: int32 [16], replicated, may hold values from 0 to 15, as said below
- pair_list: int32 [80, 2], replicated, may hold values from 0 to 15, as said below
Outputs:
- band_cross: float32 [16, 8, 2, 1024, 512], P('plane', None, None, 'pencil')
- partner_cross: float32 [16, 8, 2, 1024, 512], P('plane', None, None, 'pencil')
The draws below stay inside these ranges and needn't reach their ends.
Inputs may be any that keep to these rules, and one draw needn't show every extreme that they name: Plane q is held in slot plane_slot[q] of velocity; that slot lies in the same aligned block of 2 slots as q, and every slot holds exactly one plane. `pair_list`: each row (a, b) satisfies a <= b < a + 8; no row appears twice; rows (0, 0) and (15, 15) are present.
All inputs are finite; a program needn't handle non-finite values.
Results may differ from the reference program's by a relative error of at most 0.000088.
Values sent between devices are 32-bit elements; how exact they have to be, the bound alone decides.
A program may use at most 128 MiB of HBM per device.

```python
import math
import jax
import jax.numpy as jnp
from jax import lax

NX = 5120
NZ = 3840
KX = 512
KZ = 1024
PL_DEV = 2
PLANES = 16
BAND = 8
PAIRS = 80


def draw_plane_slot(key, part):
    blocks = PLANES // PL_DEV
    scores = jax.random.randint(key, (blocks, PL_DEV), 0, 1048576) * PL_DEV + lax.broadcasted_iota(jnp.int32, (blocks, PL_DEV), 1)
    ordering = jnp.argsort(scores, axis=1, stable=True).astype(jnp.int32)
    block_start = lax.broadcasted_iota(jnp.int32, (blocks, PL_DEV), 0) * PL_DEV
    return (block_start + ordering).reshape(PLANES).astype(jnp.int32)


def draw_pair_list(key, part):
    candidates = PLANES * BAND
    candidate = lax.broadcasted_iota(jnp.int32, (candidates,), 0)
    lower_plane = candidate // BAND
    pair_gap = candidate % BAND
    allowed = lower_plane + pair_gap < PLANES
    ceiling = 2147483647 // candidates - 2
    scores = jax.random.randint(key, (candidates,), 0, ceiling) * candidates + candidate
    forced = (candidate == 0) | (candidate == (PLANES - 1) * BAND)
    scores = jnp.where(forced, ceiling * candidates + candidate, scores)
    scores = jnp.where(allowed, scores, -1 - candidate)
    chosen = lax.top_k(scores, PAIRS)[1].astype(jnp.int32)
    return jnp.stack([chosen // BAND, chosen // BAND + chosen % BAND], axis=1).astype(jnp.int32)


def levels(rng, extent, pieces, low, top_value):
    def one(dim, blocks):
        draws = jax.random.uniform(jax.random.fold_in(jax.random.fold_in(rng, 6), dim), (blocks,), jnp.float32, low / len(pieces), top_value / len(pieces))
        return jnp.repeat(jnp.exp(draws), extent[dim] // blocks).reshape((-1,) + (1,) * (len(extent) - dim - 1))

    level = one(*pieces[0])
    for cut in pieces[1:]:
        level = level * one(*cut)
    return level


def scatter_about(own_key, extent, deviation, most, pieces=(), kind=jnp.bfloat16):
    values = deviation * jax.random.normal(own_key, extent, jnp.float32)
    if pieces:
        values = values * levels(own_key, extent, pieces, -0.22, 0.18)
    return jnp.clip(values, -most, most).astype(kind)


def setup_inputs(seed: int = 0) -> dict:
    seeds = jax.random.split(jax.random.key(seed), 4)
    velocity = scatter_about(seeds[0], (PLANES, NX, NZ), 1.0, 6.0, ((0, 8), (1, 32)), jnp.float32)
    plane_slot = draw_plane_slot(jax.random.fold_in(seeds[3], 71), 0)
    pair_list = draw_pair_list(jax.random.fold_in(seeds[3], 71), 0)
    return dict(velocity=velocity, plane_slot=plane_slot, pair_list=pair_list)


def transform_plane(field):
    along_span = jnp.fft.rfft(field, axis=1)[:, :KZ]
    both_ways = jnp.fft.fft(along_span, axis=0)
    both_ways = jnp.concatenate([both_ways[:KX // 2], both_ways[NX - KX // 2:]], axis=0)
    both_ways = jnp.transpose(both_ways) * (1.0 / math.sqrt(NX * NZ))
    return jnp.stack([jnp.real(both_ways), jnp.imag(both_ways)])

def cross_product(first, second):
    real_part = first[..., 0, :, :] * second[..., 0, :, :] + first[..., 1, :, :] * second[..., 1, :, :]
    imag_part = first[..., 1, :, :] * second[..., 0, :, :] - first[..., 0, :, :] * second[..., 1, :, :]
    return jnp.stack([real_part, imag_part], axis=-3)

def reference(velocity, plane_slot, pair_list):
    spectra_slot = lax.map(transform_plane, velocity)
    spectra = jnp.take(spectra_slot, plane_slot, axis=0)
    wanted = jnp.zeros((PLANES, BAND), jnp.int32).at[pair_list[:, 0], pair_list[:, 1] - pair_list[:, 0]].set(1)
    zero_block = jnp.zeros_like(spectra)
    conj_sign = jnp.array([1.0, -1.0], spectra.dtype).reshape(2, 1, 1)
    uppers = []
    lowers = []
    for distance in range(BAND):
        shifted_ahead = jnp.concatenate([spectra[distance:], zero_block[:distance]], axis=0)
        upper_part = jnp.where((wanted[:, distance] == 1)[:, None, None, None], cross_product(spectra, shifted_ahead), 0.0)
        lowers.append(jnp.concatenate([zero_block[:distance], (upper_part * conj_sign)[:PLANES - distance]], axis=0))
        uppers.append(upper_part)
    return (jnp.stack(uppers, axis=1), jnp.stack(lowers, axis=1))
```

```python
import functools
import math

import jax
import jax.numpy as jnp
import numpy as np
from jax import lax
from jax.experimental import pallas as pl
from jax.experimental.pallas import tpu as pltpu
from jax.sharding import PartitionSpec as P

NX = 5120
NZ = 3840
KX = 512
KZ = 1024
BAND = 8
CLASSES = 16
SPAN = NZ // CLASSES
PEERS = 32
RINGS = 8
ROWS = NX // PEERS
HALF = ROWS // 2
MESH = pl.DeviceIdType.MESH
bf16 = jnp.bfloat16
f32 = jnp.float32


def split_np(table):
    high = np.asarray(table, np.float32).astype(bf16)
    low = (table - high.astype(np.float64)).astype(np.float32).astype(bf16)
    return high, low


@functools.cache
def tables():
    lane = np.arange(128)
    t0, ri, m_lo, tb = lane // 64, lane // 32 % 2, lane // 16 % 2, lane % 16
    m = 4 * tb + 2 * t0 + m_lo
    z = np.arange(256)
    phase = 2 * np.pi * ((z[:, None] * m[None, :]) % SPAN) / SPAN
    real_rows = np.where(ri == 0, np.cos(phase), -np.sin(phase))
    imag_rows = np.where(ri == 0, np.sin(phase), np.cos(phase))
    inside = (z < SPAN)[:, None]
    span = np.concatenate([real_rows * inside, imag_rows * inside], axis=0)
    span_hi, span_lo = split_np(span)

    c = np.arange(CLASSES)
    turn = 2 * np.pi * (c[:, None] * z[None, :]) / NZ
    keep = (z < SPAN)[None, :]
    twist = np.stack([np.cos(turn) * keep, np.sin(turn) * keep], axis=1).astype(np.float32)

    k = np.arange(KX)
    kx = np.where(k < KX // 2, k, k - KX)
    r = np.arange(HALF)
    theta = 2 * np.pi * ((kx[:, None] * r[None, :]) % NX) / NX
    axial = np.concatenate([np.cos(theta), np.sin(theta)], axis=0)
    ax_hi, ax_lo = split_np(axial)
    pad = np.zeros((2 * KX, 256 - 3 * HALF), bf16)
    axial_cat = np.concatenate([ax_hi, ax_hi, ax_lo, pad], axis=1)

    step = 2 * np.pi * 2 * np.arange(16) / PEERS
    back = np.stack([np.cos(step), np.sin(step)])[:, :, None] * np.ones((1, 1, 256))
    return np.stack([span_hi, span_lo]), twist, axial_cat, back.astype(np.float32)


def times(a, w):
    ar, ai = a
    wr, wi = w
    s = math.sqrt(0.5)
    if abs(wr - 1) < 1e-12:
        return a
    if abs(wr) < 1e-12 and abs(wi + 1) < 1e-12:
        return (ai, None if ar is None else -ar)
    if abs(wr - s) < 1e-12 and abs(wi + s) < 1e-12 and ai is not None:
        return ((ar + ai) * s, (ai - ar) * s)
    if ai is None:
        return (ar * wr, ar * wi)
    return (ar * wr - ai * wi, ar * wi + ai * wr)


def add(a, b):
    if a is None:
        return b
    if b is None:
        return a
    return a + b


def sub(a, b):
    if b is None:
        return a
    if a is None:
        return -b
    return a - b


def real_fft(xs):
    n = len(xs)
    if n == 1:
        return [(xs[0], None)]
    even = real_fft(xs[0::2])
    odd = real_fft(xs[1::2])
    out = [None] * (n // 2 + 1)
    for k in range(n // 4 + 1):
        w = (math.cos(2 * math.pi * k / n), -math.sin(2 * math.pi * k / n))
        er, ei = even[k]
        tr, ti = times(odd[k], w)
        out[k] = (add(er, tr), add(ei, ti))
        if n // 2 - k != k:
            out[n // 2 - k] = (sub(er, tr), sub(ti, ei))
    return out


def twisted_classes(xs, cos_of, sin_of):
    modes = real_fft(xs)
    out = []
    for c in range(CLASSES):
        a, b = modes[c] if c <= 8 else modes[16 - c]
        if c == 0:
            out.append((a, jnp.zeros_like(a)))
            continue
        tc, ts = cos_of(c), sin_of(c)
        if b is None:
            out.append((a * tc, -(a * ts)))
        elif c < 8:
            out.append((a * tc + b * ts, b * tc - a * ts))
        else:
            out.append((a * tc - b * ts, -(b * tc + a * ts)))
    return out


def split(x):
    high = x.astype(bf16)
    return high, (x - high.astype(f32)).astype(bf16)


def lane_exchange(tiles, lane, roll):
    tiles = list(tiles)
    for bit in range(4):
        gap = 1 << bit
        low_lane = (lane & gap) == 0
        for i in range(16):
            if i & gap:
                continue
            lo, hi = tiles[i], tiles[i | gap]
            tiles[i] = jnp.where(low_lane, lo, roll(hi, gap))
            tiles[i | gap] = jnp.where(low_lane, roll(lo, 128 - gap), hi)
    return tiles


def lane_roll(x, shift):
    return pltpu.roll(x, shift, 1)


def transform_kernel(
    slot_ref, vel_hbm, span_ref, twist_ref, axial_ref, back_ref, out_ref,
    vel, y_hi, y_lo, z_buf, send_buf, recv_buf, v_cat, q_buf, acc_a, acc_b,
    load_sem, own_sem, a_send, a_recv, z_send, z_recv,
):
    me = lax.axis_index("pencil")
    ring = lax.axis_index("plane")
    below = lax.rem(ring + RINGS - 1, RINGS)
    above = lax.rem(ring + 1, RINGS)

    barrier = pltpu.get_barrier_semaphore()

    def greet(j, _):
        pl.semaphore_signal(
            barrier, inc=1, device_id=(ring, lax.rem(me + j, PEERS)), device_id_type=MESH
        )
        return 0

    for s in range(2):
        pltpu.make_async_copy(vel_hbm.at[s], vel.at[s], load_sem.at[s]).start()
    lax.fori_loop(1, PEERS, greet, 0)
    for other in (below, above):
        pl.semaphore_signal(barrier, inc=1, device_id=(other, me), device_id_type=MESH)
    v_cat[pl.ds(3 * HALF, 256 - 3 * HALF), :] = jnp.zeros((256 - 3 * HALF, 256), bf16)
    for s in range(2):
        pltpu.make_async_copy(vel_hbm.at[s], vel.at[s], load_sem.at[s]).wait()

    def spanwise(ch):
        slot = lax.rem(slot_ref[2 * ring + ch], 2)

        def residues(g, _):
            row = pl.multiple_of(g * 16, 16)
            lane = lax.broadcasted_iota(jnp.int32, (16, 128), 1)

            def tile(k):
                return vel[slot, pl.ds(row, 16), pl.ds(128 * (k % 30), 128)]

            for part in range(2):
                xs = []
                for j in range(CLASSES):
                    first, shift = divmod(SPAN * j + 128 * part, 128)
                    if shift == 0:
                        xs.append(tile(first))
                        continue
                    xs.append(
                        jnp.where(
                            lane < 128 - shift,
                            lane_roll(tile(first), 128 - shift),
                            lane_roll(tile(first + 1), 128 - shift),
                        )
                    )
                cols = pl.ds(128 * part, 128)
                cos_of = lambda c: jnp.broadcast_to(twist_ref[c, 0:1, cols], (16, 128))
                sin_of = lambda c: jnp.broadcast_to(twist_ref[c, 1:2, cols], (16, 128))
                for c, pair in enumerate(twisted_classes(xs, cos_of, sin_of)):
                    for which in range(2):
                        high, low = split(pair[which])
                        at = pl.ds(256 * which + 128 * part, 128)
                        y_hi[c, pl.ds(row, 16), at] = high
                        y_lo[c, pl.ds(row, 16), at] = low
            return 0

        lax.fori_loop(0, ROWS // 16, residues, 0)

        def products(g, _):
            high = y_hi[pl.ds(g * 4, 4)].reshape(4 * ROWS, 512)
            low = y_lo[pl.ds(g * 4, 4)].reshape(4 * ROWS, 512)
            total = jnp.dot(high, span_ref[0], preferred_element_type=f32)
            total += jnp.dot(low, span_ref[0], preferred_element_type=f32)
            total += jnp.dot(high, span_ref[1], preferred_element_type=f32)
            z_buf[pl.ds(g * 4, 4)] = total.reshape(4, ROWS, 128)
            return 0

        lax.fori_loop(0, CLASSES // 4, products, 0)

        def regroup(g, _):
            row = pl.multiple_of(g * 8, 8)
            lane = lax.broadcasted_iota(jnp.int32, (8, 128), 1)
            halves = [
                lane_exchange(
                    [z_buf[c, pl.ds(h * HALF + row, 8), :] for c in range(CLASSES)],
                    lane,
                    lane_roll,
                )
                for h in range(2)
            ]
            for tb in range(16):
                u0, u1 = halves[0][tb], halves[1][tb]
                send_buf[ch, 2 * tb, pl.ds(row, 8), :] = jnp.where(
                    lane < 64, u0, lane_roll(u1, 64)
                )
                send_buf[ch, 2 * tb + 1, pl.ds(row, 8), :] = jnp.where(
                    lane < 64, lane_roll(u0, 64), u1
                )
            return 0

        lax.fori_loop(0, HALF // 8, regroup, 0)

    def own_copy(ch):
        return pltpu.make_async_copy(
            send_buf.at[ch, me], recv_buf.at[ch, me], own_sem.at[ch]
        )

    def to_peer(ch, j):
        target = lax.rem(me + PEERS - j, PEERS)
        return pltpu.make_async_remote_copy(
            src_ref=send_buf.at[ch, target],
            dst_ref=recv_buf.at[ch, me],
            send_sem=a_send.at[ch, j],
            recv_sem=a_recv.at[ch, me],
            device_id=(ring, target),
            device_id_type=MESH,
        )

    def from_peer(ch, j):
        source = lax.rem(me + j, PEERS)
        return pltpu.make_async_remote_copy(
            src_ref=send_buf.at[ch, source],
            dst_ref=recv_buf.at[ch, source],
            send_sem=a_send.at[ch, j],
            recv_sem=a_recv.at[ch, source],
            device_id=(ring, source),
            device_id_type=MESH,
        )

    def send_all(ch):
        own_copy(ch).start()

        def one(j, _):
            to_peer(ch, j).start()
            return 0

        lax.fori_loop(1, PEERS, one, 0)

    def hop(ch, side, s):
        sign = 1 if side == 0 else -1
        return pltpu.make_async_remote_copy(
            src_ref=out_ref.at[4 + sign * (s - 1), ch],
            dst_ref=out_ref.at[4 + sign * s, ch],
            send_sem=z_send.at[ch, side, s],
            recv_sem=z_recv.at[ch, side, s],
            device_id=(below if side == 0 else above, me),
            device_id_type=MESH,
        )

    def hops_of(ch, side):
        return 4 if ch == side else 3

    def relay(ch, s):
        for side in range(2):
            if 2 <= s <= hops_of(ch, side) + 1:
                hop(ch, side, s - 1).wait_recv()
            if s <= hops_of(ch, side):
                hop(ch, side, s).start()

    def axial(ch, between):
        own_copy(ch).wait()

        def pair_step(i, _):
            @pl.when(i > 0)
            def _():
                from_peer(ch, 2 * i).wait_recv()

            from_peer(ch, 2 * i + 1).wait_recv()
            for o in range(2):
                source = lax.rem(me + 2 * i + o, PEERS)
                cols = pl.ds(128 * o, 128)
                high, low = split(recv_buf[ch, source])
                v_cat[pl.ds(0, HALF), cols] = high
                v_cat[pl.ds(HALF, HALF), cols] = low
                v_cat[pl.ds(2 * HALF, HALF), cols] = high
            q_buf[...] = jnp.dot(axial_ref[...], v_cat[...], preferred_element_type=f32)

            @pl.when(i == 0)
            def _():
                acc_a[...] = q_buf[pl.ds(0, KX), :]
                acc_b[...] = q_buf[pl.ds(KX, KX), :]

            @pl.when(i > 0)
            def _():
                cos2 = back_ref[0]
                sin2 = back_ref[1]
                for blk in range(KX // 16):
                    rows = pl.ds(16 * blk, 16)
                    a, b = acc_a[rows, :], acc_b[rows, :]
                    acc_a[rows, :] = a * cos2 + b * sin2 + q_buf[rows, :]
                    acc_b[rows, :] = b * cos2 - a * sin2 + q_buf[pl.ds(KX + 16 * blk, 16), :]

            for at, s in between:

                @pl.when(i == at)
                def _():
                    relay(0, s)

            return 0

        lax.fori_loop(0, PEERS // 2, pair_step, 0)

        k = lax.broadcasted_iota(jnp.int32, (64, 256), 0)
        lane = lax.broadcasted_iota(jnp.int32, (64, 256), 1)
        turns = lax.rem(k * (2 * (me + 30 + lane // 128) + lane // 64 % 2), 64)
        psi = turns.astype(f32) * (2.0 * math.pi / 64)
        scale = 1.0 / math.sqrt(NX * NZ)
        cos_psi = jnp.cos(psi) * scale
        sin_psi = jnp.sin(psi) * scale
        lane1 = lax.broadcasted_iota(jnp.int32, (64, 128), 1)
        for blk in range(KX // 64):
            rows = pl.ds(64 * blk, 64)
            a, b = acc_a[rows, :], acc_b[rows, :]
            pr = a * cos_psi - b * sin_psi
            qr = a * sin_psi + b * cos_psi
            pr = pr[:, :128] + pr[:, 128:]
            qr = qr[:, :128] + qr[:, 128:]
            pr = pr + lane_roll(pr, 64)
            qr = qr + lane_roll(qr, 64)
            turned = lane_roll(qr, 32)
            s_rows = pr + jnp.where(lane1 // 32 % 2 == 0, turned, -turned)
            q_buf[rows, pl.ds(0, 128)] = s_rows
        for blk in range(KX // 128):
            block = q_buf[pl.ds(128 * blk, 128), pl.ds(0, 128)]
            out_ref[4, ch, :, pl.ds(128 * blk, 128)] = block.T[:64, :]

    spanwise(0)
    pl.semaphore_wait(barrier, PEERS + 1)
    send_all(0)
    spanwise(1)
    send_all(1)
    axial(0, ())
    relay(0, 1)
    axial(1, ((4, 2), (8, 3), (12, 4)))
    relay(1, 1)
    relay(0, 5)
    for s in range(2, 6):
        relay(1, s)
    for ch in range(2):

        def sent(j, _):
            to_peer(ch, j).wait_send()
            return 0

        lax.fori_loop(1, PEERS, sent, 0)
        for side in range(2):
            for s in range(1, hops_of(ch, side) + 1):
                hop(ch, side, s).wait_send()


def cross_kernel(flag_ref, spec_ref, band_ref, partner_ref):
    ring = lax.axis_index("plane")
    own = pl.program_id(0)
    for i in range(2):

        @pl.when(own == i)
        def _():
            def pair(kz, _):
                row = pl.multiple_of(kz * 8, 8)
                re0 = spec_ref[4, i, pl.ds(row, 8), :]
                im0 = spec_ref[4, i, pl.ds(32 + row, 8), :]
                for out, sign in ((band_ref, 1), (partner_ref, -1)):
                    for d in range(BAND):
                        off, odd = divmod(i + sign * d, 2)
                        re1 = spec_ref[4 + off, odd, pl.ds(row, 8), :]
                        im1 = spec_ref[4 + off, odd, pl.ds(32 + row, 8), :]
                        which = 0 if sign == 1 else 1
                        ask = flag_ref[which, i * BAND + d] != 0
                        out[0, d, 0, pl.ds(row, 8), :] = jnp.where(
                            ask, re0 * re1 + im0 * im1, 0.0
                        )
                        out[0, d, 1, pl.ds(row, 8), :] = jnp.where(
                            ask, im0 * re1 - re0 * im1, 0.0
                        )
                return 0

            lax.fori_loop(0, 4, pair, 0)


def local(velocity, plane_slot, pair_list):
    span, twist, axial_cat, back = [jnp.asarray(t) for t in tables()]
    vmem = pl.BlockSpec(memory_space=pltpu.VMEM)
    spectra = pl.pallas_call(
        transform_kernel,
        out_shape=jax.ShapeDtypeStruct((9, 2, 64, KX), f32),
        in_specs=[
            pl.BlockSpec(memory_space=pltpu.SMEM),
            pl.BlockSpec(memory_space=pl.ANY),
            vmem,
            vmem,
            vmem,
            vmem,
        ],
        out_specs=vmem,
        scratch_shapes=[
            pltpu.VMEM((2, ROWS, NZ), f32),
            pltpu.VMEM((CLASSES, ROWS, 512), bf16),
            pltpu.VMEM((CLASSES, ROWS, 512), bf16),
            pltpu.VMEM((CLASSES, ROWS, 128), f32),
            pltpu.VMEM((2, PEERS, HALF, 128), f32),
            pltpu.VMEM((2, PEERS, HALF, 128), f32),
            pltpu.VMEM((256, 256), bf16),
            pltpu.VMEM((2 * KX, 256), f32),
            pltpu.VMEM((KX, 256), f32),
            pltpu.VMEM((KX, 256), f32),
            pltpu.SemaphoreType.DMA((2,)),
            pltpu.SemaphoreType.DMA((2,)),
            pltpu.SemaphoreType.DMA((2, PEERS)),
            pltpu.SemaphoreType.DMA((2, PEERS)),
            pltpu.SemaphoreType.DMA((2, 2, 5)),
            pltpu.SemaphoreType.DMA((2, 2, 5)),
        ],
        compiler_params=pltpu.CompilerParams(collective_id=0, has_side_effects=True),
        name="transform",
    )(plane_slot, velocity, span, twist, axial_cat, back)

    first_plane = lax.axis_index("plane") * 2
    code = pair_list[:, 0] * BAND + pair_list[:, 1] - pair_list[:, 0]
    own = first_plane + lax.broadcasted_iota(jnp.int32, (2, BAND), 0)
    gap = lax.broadcasted_iota(jnp.int32, (2, BAND), 1)
    up = own * BAND + gap
    down = jnp.where(own >= gap, (own - gap) * BAND + gap, -1)
    asked = jnp.stack([up, down]).reshape(2, 2 * BAND, 1)
    flags = jnp.any(asked == code, axis=2).astype(jnp.int32)

    share = KZ // PEERS
    out = jax.ShapeDtypeStruct((2, BAND, 2, share, KX), f32)
    block = pl.BlockSpec((1, BAND, 2, share, KX), lambda i: (i, 0, 0, 0, 0))
    band_cross, partner_cross = pl.pallas_call(
        cross_kernel,
        grid=(2,),
        out_shape=(out, out),
        in_specs=[
            pl.BlockSpec(memory_space=pltpu.SMEM),
            pl.BlockSpec((9, 2, 64, KX), lambda i: (0, 0, 0, 0)),
        ],
        out_specs=(block, block),
        name="cross",
    )(flags, spectra)
    return (band_cross, partner_cross)


def solution(mesh):
    return jax.shard_map(
        local,
        mesh=mesh,
        in_specs=(P("plane", "pencil", None), P(), P()),
        out_specs=(P("plane", None, None, "pencil", None), P("plane", None, None, "pencil", None)),
        check_vma=False,
    )
```

```python
import functools
import math

import jax
import jax.numpy as jnp
import numpy as np
from jax import lax
from jax.experimental import pallas as pl
from jax.experimental.pallas import tpu as pltpu
from jax.sharding import PartitionSpec as P

NX = 5120
NZ = 3840
KX = 512
KZ = 1024
BAND = 8
CLASSES = 16
SPAN = NZ // CLASSES
PEERS = 32
RINGS = 8
ROWS = NX // PEERS
DEPTH = 1024
MESH = pl.DeviceIdType.MESH
bf16 = jnp.bfloat16
f32 = jnp.float32


def split_np(table):
    high = np.asarray(table, np.float32).astype(bf16)
    low = (table - high.astype(np.float64)).astype(np.float32).astype(bf16)
    return high, low


@functools.cache
def tables():
    lane = np.arange(128)
    route, other, ri = lane // 8, lane // 2 % 4, lane % 2
    first, group, core = route // 8, route // 2 % 4, route % 2
    x_at = np.where(first == 0, other, group)
    y_at = np.where(first == 0, group, other)
    m = 2 * (x_at * 8 + y_at * 2 + core) + first
    z = np.arange(256)
    phase = 2 * np.pi * ((z[:, None] * m[None, :]) % SPAN) / SPAN
    real_rows = np.where(ri == 0, np.cos(phase), -np.sin(phase))
    imag_rows = np.where(ri == 0, np.sin(phase), np.cos(phase))
    inside = (z < SPAN)[:, None]
    span = np.concatenate([real_rows * inside, imag_rows * inside], axis=0)

    c = np.arange(CLASSES)
    turn = 2 * np.pi * (c[:, None] * z[None, :]) / NZ
    keep = (z < SPAN)[None, :]
    twist = np.stack([np.cos(turn) * keep, np.sin(turn) * keep], axis=1).astype(np.float32)

    k = np.arange(KX)
    kx = np.where(k < KX // 2, k, k - KX)
    r = np.arange(2 * ROWS)
    theta = 2 * np.pi * ((kx[:, None] * r[None, :]) % NX) / NX
    ax_hi, ax_lo = split_np(np.concatenate([np.cos(theta), np.sin(theta)], axis=0))
    parts = []
    for core in range(2):
        rows = slice(core * ROWS, core * ROWS + ROWS)
        parts += [ax_hi[:, rows], ax_hi[:, rows], ax_lo[:, rows]]
    parts.append(np.zeros((2 * KX, DEPTH - 6 * ROWS), bf16))
    return np.stack(split_np(span)), twist, np.concatenate(parts, axis=1)


def times(a, w):
    ar, ai = a
    wr, wi = w
    s = math.sqrt(0.5)
    if abs(wr - 1) < 1e-12:
        return a
    if abs(wr) < 1e-12 and abs(wi + 1) < 1e-12:
        return (ai, None if ar is None else -ar)
    if abs(wr - s) < 1e-12 and abs(wi + s) < 1e-12 and ai is not None:
        return ((ar + ai) * s, (ai - ar) * s)
    if ai is None:
        return (ar * wr, ar * wi)
    return (ar * wr - ai * wi, ar * wi + ai * wr)


def add(a, b):
    if a is None:
        return b
    if b is None:
        return a
    return a + b


def sub(a, b):
    if b is None:
        return a
    if a is None:
        return -b
    return a - b


def real_fft(xs):
    n = len(xs)
    if n == 1:
        return [(xs[0], None)]
    even = real_fft(xs[0::2])
    odd = real_fft(xs[1::2])
    out = [None] * (n // 2 + 1)
    for k in range(n // 4 + 1):
        w = (math.cos(2 * math.pi * k / n), -math.sin(2 * math.pi * k / n))
        er, ei = even[k]
        tr, ti = times(odd[k], w)
        out[k] = (add(er, tr), add(ei, ti))
        if n // 2 - k != k:
            out[n // 2 - k] = (sub(er, tr), sub(ti, ei))
    return out


def twisted_classes(xs, cos_of, sin_of):
    modes = real_fft(xs)
    out = []
    for c in range(CLASSES):
        a, b = modes[c] if c <= 8 else modes[16 - c]
        if c == 0:
            out.append((a, jnp.zeros_like(a)))
            continue
        tc, ts = cos_of(c), sin_of(c)
        if b is None:
            out.append((a * tc, -(a * ts)))
        elif c < 8:
            out.append((a * tc + b * ts, b * tc - a * ts))
        else:
            out.append((a * tc - b * ts, -(b * tc + a * ts)))
    return out


def split(x):
    high = x.astype(bf16)
    return high, (x - high.astype(f32)).astype(bf16)


def lane_exchange(tiles, lane, roll):
    turned = [t if c == 0 else roll(t, 8 * c) for c, t in enumerate(tiles)]
    tiles = [turned[-j % 16] for j in range(16)]
    for bit in range(4):
        gap = 1 << bit
        high_block = (lane & (8 * gap)) != 0
        tiles = [jnp.where(high_block, tiles[j - gap], tiles[j]) for j in range(16)]
    return tiles


def lane_roll(x, shift):
    return pltpu.roll(x, shift, 1)


def transform_kernel(
    slot_ref, vel_hbm, span_ref, twist_ref, axial_hbm, out_ref,
    vel, axial_ref, y_hi, y_lo, z_buf, send_buf, recv_buf, v_cat, q_buf, turn_buf,
    flip_buf, part_buf, sum_buf, load_sem, table_sem, own_sem, a_send, a_recv, b_send, b_recv,
    z_send, z_recv,
):
    me = lax.axis_index("pencil")
    ring = lax.axis_index("plane")
    below = lax.rem(ring + RINGS - 1, RINGS)
    above = lax.rem(ring + 1, RINGS)
    core = lax.rem(me, 2)
    y_at = lax.rem(me // 2, 4)
    x_at = me // 8
    place = (y_at, x_at)
    across = (x_at, y_at)

    def member(half, group, core_at):
        if half == 0:
            return x_at * 8 + group * 2 + core_at
        return group * 8 + y_at * 2 + core_at

    barrier = pltpu.get_barrier_semaphore()

    def load(slot, part):
        rows = pl.ds(part * 32, 32)
        return pltpu.make_async_copy(
            vel_hbm.at[slot, rows], vel.at[slot, rows], load_sem.at[slot, part]
        )

    for part in range(ROWS // 32):
        for slot in range(2):
            load(slot, part).start()
    tables_in = pltpu.make_async_copy(axial_hbm, axial_ref, table_sem)
    tables_in.start()
    for half in range(2):
        for step in range(4):
            for flip in range(2):
                if step == 0 and (flip == 0 or half == 1):
                    continue
                peer = member(half, lax.rem(place[half] + step, 4), lax.rem(core + flip, 2))
                pl.semaphore_signal(barrier, inc=1, device_id=(ring, peer), device_id_type=MESH)
    for other in (below, above):
        pl.semaphore_signal(barrier, inc=1, device_id=(other, me), device_id_type=MESH)
    v_cat[pl.ds(6 * ROWS, DEPTH - 6 * ROWS), :] = jnp.zeros((DEPTH - 6 * ROWS, 256), bf16)

    def spanwise(ch):
        slot = lax.rem(slot_ref[2 * ring + ch], 2)

        def residues(g, _):
            row = pl.multiple_of(g * 16, 16)
            lane = lax.broadcasted_iota(jnp.int32, (16, 128), 1)
            if ch == 0:

                @pl.when(lax.rem(g, 2) == 0)
                def _():
                    for s in range(2):
                        load(s, g // 2).wait()

            def tile(k):
                at = (pl.ds(row, 16), pl.ds(128 * (k % 30), 128))
                return jnp.where(slot == 0, vel[(0,) + at], vel[(1,) + at])

            for part in range(2):
                xs = []
                for j in range(CLASSES):
                    first, shift = divmod(SPAN * j + 128 * part, 128)
                    if shift == 0:
                        xs.append(tile(first))
                        continue
                    xs.append(
                        jnp.where(
                            lane < 128 - shift,
                            lane_roll(tile(first), 128 - shift),
                            lane_roll(tile(first + 1), 128 - shift),
                        )
                    )
                cols = pl.ds(128 * part, 128)
                cos_of = lambda c: jnp.broadcast_to(twist_ref[c, 0:1, cols], (16, 128))
                sin_of = lambda c: jnp.broadcast_to(twist_ref[c, 1:2, cols], (16, 128))
                for c, pair in enumerate(twisted_classes(xs, cos_of, sin_of)):
                    for which in range(2):
                        high, low = split(pair[which])
                        at = pl.ds(256 * which + 128 * part, 128)
                        y_hi[c, pl.ds(row, 16), at] = high
                        y_lo[c, pl.ds(row, 16), at] = low
            return 0

        lax.fori_loop(0, ROWS // 16, residues, 0)

        def products(g, _):
            high = y_hi[pl.ds(g * 4, 4)].reshape(4 * ROWS, 512)
            low = y_lo[pl.ds(g * 4, 4)].reshape(4 * ROWS, 512)
            total = jnp.dot(high, span_ref[0], preferred_element_type=f32)
            total += jnp.dot(low, span_ref[0], preferred_element_type=f32)
            total += jnp.dot(high, span_ref[1], preferred_element_type=f32)
            z_buf[pl.ds(g * 4, 4)] = total.reshape(4, ROWS, 128)
            return 0

        lax.fori_loop(0, CLASSES // 4, products, 0)

        def regroup(g, _):
            lane = lax.broadcasted_iota(jnp.int32, (8, 128), 1)
            for part in range(2):
                row = pl.multiple_of(g * 16 + part * 8, 8)
                tiles = [z_buf[c, pl.ds(row, 8), :] for c in range(CLASSES)]
                for f, tile in enumerate(lane_exchange(tiles, lane, lane_roll)):
                    send_buf[ch, f, pl.ds(row, 8), :] = tile
            return 0

        lax.fori_loop(0, ROWS // 16, regroup, 0)

    def own_copy(ch, half):
        mine = place[half] * 2 + core
        return pltpu.make_async_copy(
            send_buf.at[ch, 8 * half + mine], recv_buf.at[ch, half, mine], own_sem.at[ch, half]
        )

    def first_hop(ch, half, step, flip, back=False):
        mine = place[half] * 2 + core
        group = lax.rem(place[half] + step, 4)
        core_at = lax.rem(core + flip, 2)
        peer = group * 2 + core_at
        return pltpu.make_async_remote_copy(
            src_ref=send_buf.at[ch, 8 * half + peer],
            dst_ref=recv_buf.at[ch, half, peer if back else mine],
            send_sem=a_send.at[ch, half, 2 * step + flip],
            recv_sem=a_recv.at[ch, half, peer if back else mine],
            device_id=(ring, member(half, group, core_at)),
            device_id_type=MESH,
        )

    def second_hop(ch, half, step, back=False):
        there = lax.rem(across[half] + step, 4)
        return pltpu.make_async_remote_copy(
            src_ref=part_buf.at[ch, half, there],
            dst_ref=sum_buf.at[ch, half, there if back else across[half]],
            send_sem=b_send.at[ch, half, step],
            recv_sem=b_recv.at[ch, half, there if back else across[half]],
            device_id=(ring, member(1 - half, there, core)),
            device_id_type=MESH,
        )

    first_order = ((1, 0), (3, 0), (1, 1), (3, 1), (2, 0), (2, 1), (0, 1))

    def send_all(ch):
        for half in range(2):
            own_copy(ch, half).start()
        for step, flip in first_order:
            for half in range(2):
                first_hop(ch, half, step, flip).start()

    def hop(ch, half, side, s):
        sign = 1 if side == 0 else -1
        return pltpu.make_async_remote_copy(
            src_ref=out_ref.at[4 + sign * (s - 1), ch, half],
            dst_ref=out_ref.at[4 + sign * s, ch, half],
            send_sem=z_send.at[ch, half, side, s],
            recv_sem=z_recv.at[ch, half, side, s],
            device_id=(below if side == 0 else above, me),
            device_id_type=MESH,
        )

    def hops_of(ch, side):
        return 4 if ch == side else 3

    def relay(ch, half, s):
        for side in range(2):
            if 2 <= s <= hops_of(ch, side) + 1:
                hop(ch, half, side, s - 1).wait_recv()
            if s <= hops_of(ch, side):
                hop(ch, half, side, s).start()

    def axial(ch, half):
        own_copy(ch, half).wait()
        for step, flip in first_order:
            first_hop(ch, half, step, flip, back=True).wait_recv()

        def pair_step(s, _):
            for o in range(2):
                cols = pl.ds(128 * o, 128)
                for c in range(2):
                    high, low = split(recv_buf[ch, half, 4 * s + 2 * o + c])
                    v_cat[pl.ds(3 * c * ROWS, ROWS), cols] = high
                    v_cat[pl.ds((3 * c + 1) * ROWS, ROWS), cols] = low
                    v_cat[pl.ds((3 * c + 2) * ROWS, ROWS), cols] = high
            q_buf[s] = jnp.dot(axial_ref[...], v_cat[...], preferred_element_type=f32)
            return 0

        lax.fori_loop(0, 2, pair_step, 0)

        k = lax.broadcasted_iota(jnp.int32, (16, 256), 0)
        o = lax.broadcasted_iota(jnp.int32, (16, 256), 1) // 128
        scale = 1.0 / math.sqrt(NX * NZ)
        cos_of, sin_of = [], []
        for s in range(2):
            group = 2 * s + o
            steps = 4 * x_at + group if half == 0 else 4 * group + y_at
            psi = lax.rem(k * steps, 16).astype(f32) * (2.0 * math.pi / 16)
            cos_of.append(jnp.cos(psi) * scale)
            sin_of.append(jnp.sin(psi) * scale)
        lane = lax.broadcasted_iota(jnp.int32, (16, 128), 1)
        even = lane % 2 == 0
        mine = 8 * half + place[half] * 2 + core
        shift = lax.rem(128 - 8 * mine, 128)
        for blk in range(KX // 16):
            p = q = 0.0
            for s in range(2):
                a = q_buf[s, pl.ds(16 * blk, 16), :]
                b = q_buf[s, pl.ds(KX + 16 * blk, 16), :]
                p = p + (a * cos_of[s] - b * sin_of[s])
                q = q + (a * sin_of[s] + b * cos_of[s])
            p = p[:, :128] + p[:, 128:]
            q = q[:, :128] + q[:, 128:]
            q = jnp.where(even, -q, q)
            turn_buf[0, pl.ds(16 * blk, 16), :] = lane_roll(p, shift)
            turn_buf[1, pl.ds(16 * blk, 16), :] = lane_roll(q, shift)
        for blk in range(KX // 128):
            rows = pl.ds(128 * blk, 128)
            for which in range(2):
                flip_buf[which, blk] = turn_buf[which, rows, :].T
            for there in range(4):
                for ri in range(2):
                    straight = flip_buf[0, blk, pl.ds(2 * there + ri, 16, stride=8), :]
                    crossed = flip_buf[1, blk, pl.ds(2 * there + 1 - ri, 16, stride=8), :]
                    part_buf[ch, half, there, ri, :, rows] = straight + crossed
        for step in (1, 3, 2):
            second_hop(ch, half, step).start()

    def gather(ch, half):
        total = part_buf[ch, half, across[half]]
        for step in (1, 3, 2):
            second_hop(ch, half, step, back=True).wait_recv()
        for step in range(1, 4):
            total = total + sum_buf[ch, half, lax.rem(across[half] + step, 4)]
        out_ref[4, ch, half] = total
        relay(ch, half, 1)

    spanwise(0)
    pl.semaphore_wait(barrier, 15)
    send_all(0)
    spanwise(1)
    send_all(1)
    tables_in.wait()
    axial(0, 0)
    axial(0, 1)
    gather(0, 0)
    gather(0, 1)
    axial(1, 0)
    relay(0, 0, 2)
    relay(0, 1, 2)
    axial(1, 1)
    relay(0, 0, 3)
    relay(0, 1, 3)
    gather(1, 0)
    gather(1, 1)
    relay(0, 0, 4)
    relay(0, 1, 4)
    for s in range(2, 6):
        if s == 3:
            relay(0, 0, 5)
            relay(0, 1, 5)
        relay(1, 0, s)
        relay(1, 1, s)
    for ch in range(2):
        for half in range(2):
            for step, flip in first_order:
                first_hop(ch, half, step, flip).wait_send()
            for step in (1, 3, 2):
                second_hop(ch, half, step).wait_send()
            for side in range(2):
                for s in range(1, hops_of(ch, side) + 1):
                    hop(ch, half, side, s).wait_send()


def cross_kernel(flag_ref, spec_ref, band_ref, partner_ref):
    ring = lax.axis_index("plane")
    own = pl.program_id(0)
    for i in range(2):

        @pl.when(own == i)
        def _():
            def pair(g, _):
                half = g // 2
                row = pl.multiple_of(lax.rem(g, 2) * 8, 8)
                at = pl.multiple_of(g * 8, 8)
                re0 = spec_ref[4, i, half, 0, pl.ds(row, 8), :]
                im0 = spec_ref[4, i, half, 1, pl.ds(row, 8), :]
                for out, sign in ((band_ref, 1), (partner_ref, -1)):
                    for d in range(BAND):
                        off, odd = divmod(i + sign * d, 2)
                        re1 = spec_ref[4 + off, odd, half, 0, pl.ds(row, 8), :]
                        im1 = spec_ref[4 + off, odd, half, 1, pl.ds(row, 8), :]
                        which = 0 if sign == 1 else 1
                        ask = flag_ref[which, i * BAND + d] != 0
                        out[0, d, 0, pl.ds(at, 8), :] = jnp.where(ask, re0 * re1 + im0 * im1, 0.0)
                        out[0, d, 1, pl.ds(at, 8), :] = jnp.where(ask, im0 * re1 - re0 * im1, 0.0)
                return 0

            lax.fori_loop(0, 4, pair, 0)


def local(velocity, plane_slot, pair_list):
    span, twist, axial_cat = [jnp.asarray(t) for t in tables()]
    vmem = pl.BlockSpec(memory_space=pltpu.VMEM)
    anywhere = pl.BlockSpec(memory_space=pl.ANY)
    slab = (2, 2, 2, 16, KX)
    dma = pltpu.SemaphoreType.DMA
    spectra = pl.pallas_call(
        transform_kernel,
        out_shape=jax.ShapeDtypeStruct((9,) + slab, f32),
        in_specs=[pl.BlockSpec(memory_space=pltpu.SMEM), anywhere, vmem, vmem, anywhere],
        out_specs=vmem,
        scratch_shapes=[
            pltpu.VMEM((2, ROWS, NZ), f32),
            pltpu.VMEM((2 * KX, DEPTH), bf16),
            pltpu.VMEM((CLASSES, ROWS, 512), bf16),
            pltpu.VMEM((CLASSES, ROWS, 512), bf16),
            pltpu.VMEM((CLASSES, ROWS, 128), f32),
            pltpu.VMEM((2, CLASSES, ROWS, 128), f32),
            pltpu.VMEM((2, 2, 8, ROWS, 128), f32),
            pltpu.VMEM((DEPTH, 256), bf16),
            pltpu.VMEM((2, 2 * KX, 256), f32),
            pltpu.VMEM((2, KX, 128), f32),
            pltpu.VMEM((2, KX // 128, 128, 128), f32),
            pltpu.VMEM((2, 2, 4, 2, 16, KX), f32),
            pltpu.VMEM((2, 2, 4, 2, 16, KX), f32),
            dma((2, ROWS // 32)),
            dma,
            dma((2, 2)),
            dma((2, 2, 8)),
            dma((2, 2, 8)),
            dma((2, 2, 4)),
            dma((2, 2, 4)),
            dma((2, 2, 2, 5)),
            dma((2, 2, 2, 5)),
        ],
        compiler_params=pltpu.CompilerParams(collective_id=0, has_side_effects=True),
        name="transform",
    )(plane_slot, velocity, span, twist, axial_cat)

    first_plane = lax.axis_index("plane") * 2
    code = pair_list[:, 0] * BAND + pair_list[:, 1] - pair_list[:, 0]
    own = first_plane + lax.broadcasted_iota(jnp.int32, (2, BAND), 0)
    gap = lax.broadcasted_iota(jnp.int32, (2, BAND), 1)
    up = own * BAND + gap
    down = jnp.where(own >= gap, (own - gap) * BAND + gap, -1)
    asked = jnp.stack([up, down]).reshape(2, 2 * BAND, 1)
    flags = jnp.any(asked == code, axis=2).astype(jnp.int32)

    share = KZ // PEERS
    out = jax.ShapeDtypeStruct((2, BAND, 2, share, KX), f32)
    block = pl.BlockSpec((1, BAND, 2, share, KX), lambda i: (i, 0, 0, 0, 0))
    band_cross, partner_cross = pl.pallas_call(
        cross_kernel,
        grid=(2,),
        out_shape=(out, out),
        in_specs=[
            pl.BlockSpec(memory_space=pltpu.SMEM),
            pl.BlockSpec((9,) + slab, lambda i: (0,) * 6),
        ],
        out_specs=(block, block),
        name="cross",
    )(flags, spectra)
    return (band_cross, partner_cross)


def solution(mesh):
    return jax.shard_map(
        local,
        mesh=mesh,
        in_specs=(P("plane", "pencil", None), P(), P()),
        out_specs=(P("plane", None, None, "pencil", None), P("plane", None, None, "pencil", None)),
        check_vma=False,
    )
```

```python
import functools
import math

import jax
import jax.numpy as jnp
import numpy as np
from jax import lax
from jax.experimental import pallas as pl
from jax.experimental.pallas import tpu as pltpu
from jax.sharding import PartitionSpec as P

NX = 5120
NZ = 3840
KX = 512
KZ = 1024
BAND = 8
CLASSES = 16
SPAN = NZ // CLASSES
PEERS = 32
RINGS = 8
ROWS = NX // PEERS
DEPTH = 1024
MESH = pl.DeviceIdType.MESH
bf16 = jnp.bfloat16
f32 = jnp.float32


def split_np(table):
    high = np.asarray(table, np.float32).astype(bf16)
    low = (table - high.astype(np.float64)).astype(np.float32).astype(bf16)
    return high, low


@functools.cache
def tables():
    lane = np.arange(128)
    route, other, ri = lane // 8, lane // 2 % 4, lane % 2
    first, group, core = route // 8, route // 2 % 4, route % 2
    x_at = np.where(first == 0, other, group)
    y_at = np.where(first == 0, group, other)
    m = 2 * (x_at * 8 + y_at * 2 + core) + first
    z = np.arange(256)
    phase = 2 * np.pi * ((z[:, None] * m[None, :]) % SPAN) / SPAN
    real_rows = np.where(ri == 0, np.cos(phase), -np.sin(phase))
    imag_rows = np.where(ri == 0, np.sin(phase), np.cos(phase))
    inside = (z < SPAN)[:, None]
    span = np.concatenate([real_rows * inside, imag_rows * inside], axis=0)

    c = np.arange(CLASSES)
    turn = 2 * np.pi * (c[:, None] * z[None, :]) / NZ
    keep = (z < SPAN)[None, :]
    twist = np.stack([np.cos(turn) * keep, np.sin(turn) * keep], axis=1).astype(np.float32)

    k = np.arange(KX)
    kx = np.where(k < KX // 2, k, k - KX)
    r = np.arange(2 * ROWS)
    theta = 2 * np.pi * ((kx[:, None] * r[None, :]) % NX) / NX
    ax_hi, ax_lo = split_np(np.concatenate([np.cos(theta), np.sin(theta)], axis=0))
    parts = []
    for core in range(2):
        rows = slice(core * ROWS, core * ROWS + ROWS)
        parts += [ax_hi[:, rows], ax_hi[:, rows], ax_lo[:, rows]]
    parts.append(np.zeros((2 * KX, DEPTH - 6 * ROWS), bf16))
    return np.stack(split_np(span)), twist, np.concatenate(parts, axis=1)


def times(a, w):
    ar, ai = a
    wr, wi = w
    s = math.sqrt(0.5)
    if abs(wr - 1) < 1e-12:
        return a
    if abs(wr) < 1e-12 and abs(wi + 1) < 1e-12:
        return (ai, None if ar is None else -ar)
    if abs(wr - s) < 1e-12 and abs(wi + s) < 1e-12 and ai is not None:
        return ((ar + ai) * s, (ai - ar) * s)
    if ai is None:
        return (ar * wr, ar * wi)
    return (ar * wr - ai * wi, ar * wi + ai * wr)


def add(a, b):
    if a is None:
        return b
    if b is None:
        return a
    return a + b


def sub(a, b):
    if b is None:
        return a
    if a is None:
        return -b
    return a - b


def real_fft(xs):
    n = len(xs)
    if n == 1:
        return [(xs[0], None)]
    even = real_fft(xs[0::2])
    odd = real_fft(xs[1::2])
    out = [None] * (n // 2 + 1)
    for k in range(n // 4 + 1):
        w = (math.cos(2 * math.pi * k / n), -math.sin(2 * math.pi * k / n))
        er, ei = even[k]
        tr, ti = times(odd[k], w)
        out[k] = (add(er, tr), add(ei, ti))
        if n // 2 - k != k:
            out[n // 2 - k] = (sub(er, tr), sub(ti, ei))
    return out


def twisted_classes(xs, cos_of, sin_of):
    modes = real_fft(xs)
    out = []
    for c in range(CLASSES):
        a, b = modes[c] if c <= 8 else modes[16 - c]
        if c == 0:
            out.append((a, jnp.zeros_like(a)))
            continue
        tc, ts = cos_of(c), sin_of(c)
        if b is None:
            out.append((a * tc, -(a * ts)))
        elif c < 8:
            out.append((a * tc + b * ts, b * tc - a * ts))
        else:
            out.append((a * tc - b * ts, -(b * tc + a * ts)))
    return out


def split(x):
    high = x.astype(bf16)
    return high, (x - high.astype(f32)).astype(bf16)


def lane_exchange(tiles, lane, roll):
    turned = [t if c == 0 else roll(t, 8 * c) for c, t in enumerate(tiles)]
    tiles = [turned[-j % 16] for j in range(16)]
    for bit in range(4):
        gap = 1 << bit
        high_block = (lane & (8 * gap)) != 0
        tiles = [jnp.where(high_block, tiles[j - gap], tiles[j]) for j in range(16)]
    return tiles


def lane_roll(x, shift):
    return pltpu.roll(x, shift, 1)


def transform_kernel(
    slot_ref, vel_hbm, span_ref, twist_ref, axial_hbm, out_ref,
    vel, axial_ref, hi_even, lo_even, hi_odd, lo_odd, z_even, z_odd, send_buf, recv_buf, v_cat, q_buf, turn_buf,
    flip_buf, part_buf, sum_buf, load_sem, table_sem, own_sem, a_send, a_recv, b_send, b_recv,
    z_send, z_recv,
):
    me = lax.axis_index("pencil")
    ring = lax.axis_index("plane")
    below = lax.rem(ring + RINGS - 1, RINGS)
    above = lax.rem(ring + 1, RINGS)
    core = lax.rem(me, 2)
    y_at = lax.rem(me // 2, 4)
    x_at = me // 8
    place = (y_at, x_at)
    across = (x_at, y_at)

    def member(half, group, core_at):
        if half == 0:
            return x_at * 8 + group * 2 + core_at
        return group * 8 + y_at * 2 + core_at

    barrier = pltpu.get_barrier_semaphore()

    def load(slot, part):
        rows = pl.ds(part * 32, 32)
        return pltpu.make_async_copy(
            vel_hbm.at[slot, rows], vel.at[slot, rows], load_sem.at[slot, part]
        )

    for part in range(ROWS // 32):
        for slot in range(2):
            load(slot, part).start()
    tables_in = pltpu.make_async_copy(axial_hbm, axial_ref, table_sem)
    tables_in.start()
    for half in range(2):
        for step in range(4):
            for flip in range(2):
                if step == 0 and (flip == 0 or half == 1):
                    continue
                peer = member(half, lax.rem(place[half] + step, 4), lax.rem(core + flip, 2))
                pl.semaphore_signal(barrier, inc=1, device_id=(ring, peer), device_id_type=MESH)
    for other in (below, above):
        pl.semaphore_signal(barrier, inc=1, device_id=(other, me), device_id_type=MESH)
    v_cat[pl.ds(6 * ROWS, DEPTH - 6 * ROWS), :] = jnp.zeros((DEPTH - 6 * ROWS, 256), bf16)

    lane16 = lax.broadcasted_iota(jnp.int32, (16, 128), 1)
    lane8 = lax.broadcasted_iota(jnp.int32, (8, 128), 1)
    groups = ROWS // 16

    def residues(g, y_hi, y_lo):
        slot = lax.rem(slot_ref[2 * ring + g // groups], 2)
        row = pl.multiple_of(lax.rem(g, groups) * 16, 16)

        def tile(k):
            at = (pl.ds(row, 16), pl.ds(128 * (k % 30), 128))
            return jnp.where(slot == 0, vel[(0,) + at], vel[(1,) + at])

        for part in range(2):
            xs = []
            for j in range(CLASSES):
                first, shift = divmod(SPAN * j + 128 * part, 128)
                if shift == 0:
                    xs.append(tile(first))
                    continue
                xs.append(
                    jnp.where(
                        lane16 < 128 - shift,
                        lane_roll(tile(first), 128 - shift),
                        lane_roll(tile(first + 1), 128 - shift),
                    )
                )
            cols = pl.ds(128 * part, 128)
            cos_of = lambda c: jnp.broadcast_to(twist_ref[c, 0:1, cols], (16, 128))
            sin_of = lambda c: jnp.broadcast_to(twist_ref[c, 1:2, cols], (16, 128))
            for c, pair in enumerate(twisted_classes(xs, cos_of, sin_of)):
                for which in range(2):
                    high, low = split(pair[which])
                    at = pl.ds(256 * which + 128 * part, 128)
                    y_hi[c, :, at] = high
                    y_lo[c, :, at] = low

    def products(y_hi, y_lo, z_buf):
        high = y_hi[...].reshape(CLASSES * 16, 512)
        low = y_lo[...].reshape(CLASSES * 16, 512)
        total = jnp.dot(high, span_ref[0], preferred_element_type=f32)
        total += jnp.dot(low, span_ref[0], preferred_element_type=f32)
        total += jnp.dot(high, span_ref[1], preferred_element_type=f32)
        z_buf[...] = total.reshape(CLASSES, 16, 128)

    def regroup(g, z_buf):
        g = jnp.maximum(g, 0)
        row = pl.multiple_of(lax.rem(g, groups) * 16, 16)
        for part in range(2):
            tiles = [z_buf[c, pl.ds(8 * part, 8), :] for c in range(CLASSES)]
            for f, tile in enumerate(lane_exchange(tiles, lane8, lane_roll)):
                send_buf[g // groups, f, pl.ds(row + 8 * part, 8), :] = tile

    def own_copy(ch, half):
        mine = place[half] * 2 + core
        return pltpu.make_async_copy(
            send_buf.at[ch, 8 * half + mine], recv_buf.at[ch, half, mine], own_sem.at[ch, half]
        )

    def first_hop(ch, half, step, flip, back=False, rows=pl.ds(0, ROWS)):
        mine = place[half] * 2 + core
        group = lax.rem(place[half] + step, 4)
        core_at = lax.rem(core + flip, 2)
        peer = group * 2 + core_at
        return pltpu.make_async_remote_copy(
            src_ref=send_buf.at[ch, 8 * half + peer, rows],
            dst_ref=recv_buf.at[ch, half, peer if back else mine, rows],
            send_sem=a_send.at[ch, half, 2 * step + flip],
            recv_sem=a_recv.at[ch, half, peer if back else mine],
            device_id=(ring, member(half, group, core_at)),
            device_id_type=MESH,
        )

    def second_hop(ch, half, step, back=False):
        there = lax.rem(across[half] + step, 4)
        return pltpu.make_async_remote_copy(
            src_ref=part_buf.at[ch, half, there],
            dst_ref=sum_buf.at[ch, half, there if back else across[half]],
            send_sem=b_send.at[ch, half, step],
            recv_sem=b_recv.at[ch, half, there if back else across[half]],
            device_id=(ring, member(1 - half, there, core)),
            device_id_type=MESH,
        )

    first_order = ((1, 0), (3, 0), (1, 1), (3, 1), (2, 0), (2, 1), (0, 1))

    parts = (pl.ds(0, 96), pl.ds(96, 64))

    def send_part(ch, part):
        if part == 1:
            for half in range(2):
                own_copy(ch, half).start()
        for step, flip in first_order:
            for half in range(2):
                first_hop(ch, half, step, flip, rows=parts[part]).start()

    def hop(ch, half, side, s):
        sign = 1 if side == 0 else -1
        return pltpu.make_async_remote_copy(
            src_ref=out_ref.at[4 + sign * (s - 1), ch, half],
            dst_ref=out_ref.at[4 + sign * s, ch, half],
            send_sem=z_send.at[ch, half, side, s],
            recv_sem=z_recv.at[ch, half, side, s],
            device_id=(below if side == 0 else above, me),
            device_id_type=MESH,
        )

    def hops_of(ch, side):
        return 4 if ch == side else 3

    def relay(ch, half, s):
        for side in range(2):
            if 2 <= s <= hops_of(ch, side) + 1:
                hop(ch, half, side, s - 1).wait_recv()
            if s <= hops_of(ch, side):
                hop(ch, half, side, s).start()

    def axial(ch, half):
        own_copy(ch, half).wait()
        for step, flip in first_order:
            first_hop(ch, half, step, flip, back=True).wait_recv()

        def pair_step(s, _):
            for o in range(2):
                cols = pl.ds(128 * o, 128)
                for c in range(2):
                    high, low = split(recv_buf[ch, half, 4 * s + 2 * o + c])
                    v_cat[pl.ds(3 * c * ROWS, ROWS), cols] = high
                    v_cat[pl.ds((3 * c + 1) * ROWS, ROWS), cols] = low
                    v_cat[pl.ds((3 * c + 2) * ROWS, ROWS), cols] = high
            q_buf[s] = jnp.dot(axial_ref[...], v_cat[...], preferred_element_type=f32)
            return 0

        lax.fori_loop(0, 2, pair_step, 0)

        k = lax.broadcasted_iota(jnp.int32, (16, 256), 0)
        o = lax.broadcasted_iota(jnp.int32, (16, 256), 1) // 128
        scale = 1.0 / math.sqrt(NX * NZ)
        cos_of, sin_of = [], []
        for s in range(2):
            group = 2 * s + o
            steps = 4 * x_at + group if half == 0 else 4 * group + y_at
            psi = lax.rem(k * steps, 16).astype(f32) * (2.0 * math.pi / 16)
            cos_of.append(jnp.cos(psi) * scale)
            sin_of.append(jnp.sin(psi) * scale)
        lane = lax.broadcasted_iota(jnp.int32, (16, 128), 1)
        even = lane % 2 == 0
        mine = 8 * half + place[half] * 2 + core
        shift = lax.rem(128 - 8 * mine, 128)
        for blk in range(KX // 16):
            p = q = 0.0
            for s in range(2):
                a = q_buf[s, pl.ds(16 * blk, 16), :]
                b = q_buf[s, pl.ds(KX + 16 * blk, 16), :]
                p = p + (a * cos_of[s] - b * sin_of[s])
                q = q + (a * sin_of[s] + b * cos_of[s])
            p = p[:, :128] + p[:, 128:]
            q = q[:, :128] + q[:, 128:]
            q = jnp.where(even, -q, q)
            turn_buf[0, pl.ds(16 * blk, 16), :] = lane_roll(p, shift)
            turn_buf[1, pl.ds(16 * blk, 16), :] = lane_roll(q, shift)
        for blk in range(KX // 128):
            rows = pl.ds(128 * blk, 128)
            for which in range(2):
                flip_buf[which, blk] = turn_buf[which, rows, :].T
            for there in range(4):
                for ri in range(2):
                    straight = flip_buf[0, blk, pl.ds(2 * there + ri, 16, stride=8), :]
                    crossed = flip_buf[1, blk, pl.ds(2 * there + 1 - ri, 16, stride=8), :]
                    part_buf[ch, half, there, ri, :, rows] = straight + crossed
        for step in (1, 3, 2):
            second_hop(ch, half, step).start()

    def gather(ch, half):
        total = part_buf[ch, half, across[half]]
        for step in (1, 3, 2):
            second_hop(ch, half, step, back=True).wait_recv()
        for step in range(1, 4):
            total = total + sum_buf[ch, half, lax.rem(across[half] + step, 4)]
        out_ref[4, ch, half] = total
        relay(ch, half, 1)

    def body(q, _):
        @pl.when(q < groups // 2)
        def _():
            for s in range(2):
                load(s, q).wait()

        for odd in range(2):
            regroup(2 * q + odd - 2, (z_even, z_odd)[odd])
            if odd == 0:
                products(hi_odd, lo_odd, z_odd)
                residues(2 * q, hi_even, lo_even)
            else:
                products(hi_even, lo_even, z_even)
                residues(2 * q + 1, hi_odd, lo_odd)

        @pl.when(q == 3)
        def _():
            pl.semaphore_wait(barrier, 15)
            send_part(0, 0)

        @pl.when(q == 5)
        def _():
            send_part(0, 1)

        @pl.when(q == 8)
        def _():
            send_part(1, 0)

        return 0

    lax.fori_loop(0, groups, body, 0)
    regroup(2 * groups - 2, z_even)
    products(hi_odd, lo_odd, z_odd)
    regroup(2 * groups - 1, z_odd)
    tables_in.wait()
    axial(0, 0)
    axial(0, 1)
    send_part(1, 1)
    gather(0, 0)
    gather(0, 1)
    axial(1, 0)
    relay(0, 0, 2)
    relay(0, 1, 2)
    axial(1, 1)
    relay(0, 0, 3)
    relay(0, 1, 3)
    gather(1, 0)
    gather(1, 1)
    relay(0, 0, 4)
    relay(0, 1, 4)
    for s in range(2, 6):
        if s == 3:
            relay(0, 0, 5)
            relay(0, 1, 5)
        relay(1, 0, s)
        relay(1, 1, s)
    for ch in range(2):
        for half in range(2):
            for step, flip in first_order:
                first_hop(ch, half, step, flip).wait_send()
            for step in (1, 3, 2):
                second_hop(ch, half, step).wait_send()
            for side in range(2):
                for s in range(1, hops_of(ch, side) + 1):
                    hop(ch, half, side, s).wait_send()


def cross_kernel(flag_ref, spec_ref, band_ref, partner_ref):
    ring = lax.axis_index("plane")
    own = pl.program_id(0)
    for i in range(2):

        @pl.when(own == i)
        def _():
            def pair(g, _):
                half = g // 2
                row = pl.multiple_of(lax.rem(g, 2) * 8, 8)
                at = pl.multiple_of(g * 8, 8)
                re0 = spec_ref[4, i, half, 0, pl.ds(row, 8), :]
                im0 = spec_ref[4, i, half, 1, pl.ds(row, 8), :]
                for out, sign in ((band_ref, 1), (partner_ref, -1)):
                    for d in range(BAND):
                        off, odd = divmod(i + sign * d, 2)
                        re1 = spec_ref[4 + off, odd, half, 0, pl.ds(row, 8), :]
                        im1 = spec_ref[4 + off, odd, half, 1, pl.ds(row, 8), :]
                        which = 0 if sign == 1 else 1
                        ask = flag_ref[which, i * BAND + d] != 0
                        out[0, d, 0, pl.ds(at, 8), :] = jnp.where(ask, re0 * re1 + im0 * im1, 0.0)
                        out[0, d, 1, pl.ds(at, 8), :] = jnp.where(ask, im0 * re1 - re0 * im1, 0.0)
                return 0

            lax.fori_loop(0, 4, pair, 0)


def local(velocity, plane_slot, pair_list):
    span, twist, axial_cat = [jnp.asarray(t) for t in tables()]
    vmem = pl.BlockSpec(memory_space=pltpu.VMEM)
    anywhere = pl.BlockSpec(memory_space=pl.ANY)
    slab = (2, 2, 2, 16, KX)
    dma = pltpu.SemaphoreType.DMA
    spectra = pl.pallas_call(
        transform_kernel,
        out_shape=jax.ShapeDtypeStruct((9,) + slab, f32),
        in_specs=[pl.BlockSpec(memory_space=pltpu.SMEM), anywhere, vmem, vmem, anywhere],
        out_specs=vmem,
        scratch_shapes=[
            pltpu.VMEM((2, ROWS, NZ), f32),
            pltpu.VMEM((2 * KX, DEPTH), bf16),
            pltpu.VMEM((CLASSES, 16, 512), bf16),
            pltpu.VMEM((CLASSES, 16, 512), bf16),
            pltpu.VMEM((CLASSES, 16, 512), bf16),
            pltpu.VMEM((CLASSES, 16, 512), bf16),
            pltpu.VMEM((CLASSES, 16, 128), f32),
            pltpu.VMEM((CLASSES, 16, 128), f32),
            pltpu.VMEM((2, CLASSES, ROWS, 128), f32),
            pltpu.VMEM((2, 2, 8, ROWS, 128), f32),
            pltpu.VMEM((DEPTH, 256), bf16),
            pltpu.VMEM((2, 2 * KX, 256), f32),
            pltpu.VMEM((2, KX, 128), f32),
            pltpu.VMEM((2, KX // 128, 128, 128), f32),
            pltpu.VMEM((2, 2, 4, 2, 16, KX), f32),
            pltpu.VMEM((2, 2, 4, 2, 16, KX), f32),
            dma((2, ROWS // 32)),
            dma,
            dma((2, 2)),
            dma((2, 2, 8)),
            dma((2, 2, 8)),
            dma((2, 2, 4)),
            dma((2, 2, 4)),
            dma((2, 2, 2, 5)),
            dma((2, 2, 2, 5)),
        ],
        compiler_params=pltpu.CompilerParams(collective_id=0, has_side_effects=True),
        name="transform",
    )(plane_slot, velocity, span, twist, axial_cat)

    first_plane = lax.axis_index("plane") * 2
    code = pair_list[:, 0] * BAND + pair_list[:, 1] - pair_list[:, 0]
    own = first_plane + lax.broadcasted_iota(jnp.int32, (2, BAND), 0)
    gap = lax.broadcasted_iota(jnp.int32, (2, BAND), 1)
    up = own * BAND + gap
    down = jnp.where(own >= gap, (own - gap) * BAND + gap, -1)
    asked = jnp.stack([up, down]).reshape(2, 2 * BAND, 1)
    flags = jnp.any(asked == code, axis=2).astype(jnp.int32)

    share = KZ // PEERS
    out = jax.ShapeDtypeStruct((2, BAND, 2, share, KX), f32)
    block = pl.BlockSpec((1, BAND, 2, share, KX), lambda i: (i, 0, 0, 0, 0))
    band_cross, partner_cross = pl.pallas_call(
        cross_kernel,
        grid=(2,),
        out_shape=(out, out),
        in_specs=[
            pl.BlockSpec(memory_space=pltpu.SMEM),
            pl.BlockSpec((9,) + slab, lambda i: (0,) * 6),
        ],
        out_specs=(block, block),
        name="cross",
    )(flags, spectra)
    return (band_cross, partner_cross)


def solution(mesh):
    return jax.shard_map(
        local,
        mesh=mesh,
        in_specs=(P("plane", "pencil", None), P(), P()),
        out_specs=(P("plane", None, None, "pencil", None), P("plane", None, None, "pencil", None)),
        check_vma=False,
    )
```

```python
import functools
import math

import jax
import jax.numpy as jnp
import numpy as np
from jax import lax
from jax.experimental import pallas as pl
from jax.experimental.pallas import tpu as pltpu
from jax.sharding import PartitionSpec as P

NX = 5120
NZ = 3840
KX = 512
KZ = 1024
BAND = 8
CLASSES = 16
SPAN = NZ // CLASSES
PEERS = 32
RINGS = 8
ROWS = NX // PEERS
DEPTH = 1024
MESH = pl.DeviceIdType.MESH
bf16 = jnp.bfloat16
f32 = jnp.float32


def split_np(table):
    high = np.asarray(table, np.float32).astype(bf16)
    low = (table - high.astype(np.float64)).astype(np.float32).astype(bf16)
    return high, low


@functools.cache
def tables():
    lane = np.arange(128)
    route, other, ri = lane // 8, lane // 2 % 4, lane % 2
    first, group, core = route // 8, route // 2 % 4, route % 2
    x_at = np.where(first == 0, other, group)
    y_at = np.where(first == 0, group, other)
    m = 2 * (x_at * 8 + y_at * 2 + core) + first
    z = np.arange(256)
    phase = 2 * np.pi * ((z[:, None] * m[None, :]) % SPAN) / SPAN
    real_rows = np.where(ri == 0, np.cos(phase), -np.sin(phase))
    imag_rows = np.where(ri == 0, np.sin(phase), np.cos(phase))
    inside = (z < SPAN)[:, None]
    span = np.concatenate([real_rows * inside, imag_rows * inside], axis=0)

    c = np.arange(CLASSES)
    turn = 2 * np.pi * (c[:, None] * z[None, :]) / NZ
    keep = (z < SPAN)[None, :]
    twist = np.stack([np.cos(turn) * keep, np.sin(turn) * keep], axis=1).astype(np.float32)

    k = np.arange(KX)
    kx = np.where(k < KX // 2, k, k - KX)
    r = np.arange(2 * ROWS)
    theta = 2 * np.pi * ((kx[:, None] * r[None, :]) % NX) / NX
    ax_hi, ax_lo = split_np(np.concatenate([np.cos(theta), np.sin(theta)], axis=0))
    parts = []
    for core in range(2):
        rows = slice(core * ROWS, core * ROWS + ROWS)
        parts += [ax_hi[:, rows], ax_hi[:, rows], ax_lo[:, rows]]
    parts.append(np.zeros((2 * KX, DEPTH - 6 * ROWS), bf16))
    axial = np.concatenate(parts, axis=1).reshape(2, 2, KX // 2, DEPTH)
    axial = np.ascontiguousarray(axial.transpose(1, 0, 2, 3)).reshape(2, KX, DEPTH)
    return np.stack(split_np(span)), twist, axial


def times(a, w):
    ar, ai = a
    wr, wi = w
    s = math.sqrt(0.5)
    if abs(wr - 1) < 1e-12:
        return a
    if abs(wr) < 1e-12 and abs(wi + 1) < 1e-12:
        return (ai, None if ar is None else -ar)
    if abs(wr - s) < 1e-12 and abs(wi + s) < 1e-12 and ai is not None:
        return ((ar + ai) * s, (ai - ar) * s)
    if ai is None:
        return (ar * wr, ar * wi)
    return (ar * wr - ai * wi, ar * wi + ai * wr)


def add(a, b):
    if a is None:
        return b
    if b is None:
        return a
    return a + b


def sub(a, b):
    if b is None:
        return a
    if a is None:
        return -b
    return a - b


def real_fft(xs):
    n = len(xs)
    if n == 1:
        return [(xs[0], None)]
    even = real_fft(xs[0::2])
    odd = real_fft(xs[1::2])
    out = [None] * (n // 2 + 1)
    for k in range(n // 4 + 1):
        w = (math.cos(2 * math.pi * k / n), -math.sin(2 * math.pi * k / n))
        er, ei = even[k]
        tr, ti = times(odd[k], w)
        out[k] = (add(er, tr), add(ei, ti))
        if n // 2 - k != k:
            out[n // 2 - k] = (sub(er, tr), sub(ti, ei))
    return out


def twisted_pair(modes, i, cos_of, sin_of):
    stack = lambda u, v: jnp.concatenate([u, v], axis=0)
    a, b = modes[i]
    if i == 0:
        e = modes[8][0]
        return stack(a, e * cos_of(8)), stack(jnp.zeros_like(a), -(e * sin_of(8)))
    tc, ts = cos_of(i), sin_of(i)
    uc, us = cos_of(16 - i), sin_of(16 - i)
    return stack(a * tc + b * ts, a * uc - b * us), stack(b * tc - a * ts, -(b * uc + a * us))


def split(x):
    high = x.astype(bf16)
    return high, (x - high.astype(f32)).astype(bf16)


def lane_exchange(tiles, lane, roll):
    turned = [t if c == 0 else roll(t, 8 * c) for c, t in enumerate(tiles)]
    tiles = [turned[-j % 16] for j in range(16)]
    for bit in range(4):
        gap = 1 << bit
        high_block = (lane & (8 * gap)) != 0
        tiles = [jnp.where(high_block, tiles[j - gap], tiles[j]) for j in range(16)]
    return tiles


def lane_roll(x, shift):
    return pltpu.roll(x, shift, 1)


def transform_kernel(
    slot_ref, vel_hbm, span_ref, twist_ref, axial_hbm, out_ref,
    vel, axial_ref, hi_even, lo_even, hi_odd, lo_odd, z_even, z_odd, send_buf, recv_buf, v_cat, q_buf, turn_buf,
    flip_buf, part_buf, sum_buf, load_sem, table_sem, own_sem, a_send, a_recv, b_send, b_recv,
    z_send, z_recv,
):
    me = lax.axis_index("pencil")
    ring = lax.axis_index("plane")
    below = lax.rem(ring + RINGS - 1, RINGS)
    above = lax.rem(ring + 1, RINGS)
    core = lax.rem(me, 2)
    y_at = lax.rem(me // 2, 4)
    x_at = me // 8
    place = (y_at, x_at)
    across = (x_at, y_at)

    def member(half, group, core_at):
        if half == 0:
            return x_at * 8 + group * 2 + core_at
        return group * 8 + y_at * 2 + core_at

    barrier = pltpu.get_barrier_semaphore()

    def load(slot, part):
        rows = pl.ds(part * 32, 32)
        return pltpu.make_async_copy(
            vel_hbm.at[slot, rows], vel.at[slot, rows], load_sem.at[slot, part]
        )

    for part in range(ROWS // 32):
        for slot in range(2):
            load(slot, part).start()
    tables_in = pltpu.make_async_copy(axial_hbm, axial_ref, table_sem)
    tables_in.start()
    for half in range(2):
        for step in range(4):
            for flip in range(2):
                if step == 0 and (flip == 0 or half == 1):
                    continue
                peer = member(half, lax.rem(place[half] + step, 4), lax.rem(core + flip, 2))
                pl.semaphore_signal(barrier, inc=1, device_id=(ring, peer), device_id_type=MESH)
    for other in (below, above):
        pl.semaphore_signal(barrier, inc=1, device_id=(other, me), device_id_type=MESH)
    for half in range(2):
        for s in range(2):
            rest = pl.ds(6 * ROWS, DEPTH - 6 * ROWS)
            v_cat[half, s, rest, :] = jnp.zeros((DEPTH - 6 * ROWS, 256), bf16)

    lane8 = lax.broadcasted_iota(jnp.int32, (8, 128), 1)
    groups = ROWS // 16

    def residues(g, y_hi, y_lo):
        slot = lax.rem(slot_ref[2 * ring + g // groups], 2)
        row = pl.multiple_of(lax.rem(g, groups) * 16, 16)

        def tile(k, half):
            at = (pl.ds(row + 8 * half, 8), pl.ds(128 * (k % 30), 128))
            return jnp.where(slot == 0, vel[(0,) + at], vel[(1,) + at])

        for part, half in ((0, 0), (0, 1), (1, 0), (1, 1)):
            xs = []
            for j in range(CLASSES):
                first, shift = divmod(SPAN * j + 128 * part, 128)
                if shift == 0:
                    xs.append(tile(first, half))
                    continue
                xs.append(
                    jnp.where(
                        lane8 < 128 - shift,
                        lane_roll(tile(first, half), 128 - shift),
                        lane_roll(tile(first + 1, half), 128 - shift),
                    )
                )
            cols = pl.ds(128 * part, 128)
            cos_of = lambda c: jnp.broadcast_to(twist_ref[c, 0:1, cols], (8, 128))
            sin_of = lambda c: jnp.broadcast_to(twist_ref[c, 1:2, cols], (8, 128))
            modes = real_fft(xs)
            for i in range(8):
                for which, value in enumerate(twisted_pair(modes, i, cos_of, sin_of)):
                    at = pl.ds(256 * which + 128 * part, 128)
                    y_hi[half, i, :, at], y_lo[half, i, :, at] = split(value)

    def products(y_hi, y_lo, z_buf):
        high = y_hi[...].reshape(CLASSES * 16, 512)
        low = y_lo[...].reshape(CLASSES * 16, 512)
        total = jnp.dot(high, span_ref[0], preferred_element_type=f32)
        total += jnp.dot(low, span_ref[0], preferred_element_type=f32)
        total += jnp.dot(high, span_ref[1], preferred_element_type=f32)
        z_buf[...] = total.reshape(2, 8, 16, 128)

    def regroup(g, z_buf):
        g = jnp.maximum(g, 0)
        row = pl.multiple_of(lax.rem(g, groups) * 16, 16)
        for part in range(2):
            tiles = [z_buf[part, min(c, 16 - c) % 8, pl.ds(c // 8 * 8, 8), :] for c in range(CLASSES)]
            for f, tile in enumerate(lane_exchange(tiles, lane8, lane_roll)):
                send_buf[g // groups, f, pl.ds(row + 8 * part, 8), :] = tile

    def own_copy(ch, half):
        mine = place[half] * 2 + core
        return pltpu.make_async_copy(
            send_buf.at[ch, 8 * half + mine], recv_buf.at[ch, half, mine], own_sem.at[ch, half]
        )

    def first_hop(ch, half, step, flip, back=False, rows=pl.ds(0, ROWS)):
        mine = place[half] * 2 + core
        group = lax.rem(place[half] + step, 4)
        core_at = lax.rem(core + flip, 2)
        peer = group * 2 + core_at
        return pltpu.make_async_remote_copy(
            src_ref=send_buf.at[ch, 8 * half + peer, rows],
            dst_ref=recv_buf.at[ch, half, peer if back else mine, rows],
            send_sem=a_send.at[ch, half, 2 * step + flip],
            recv_sem=a_recv.at[ch, half, peer if back else mine],
            device_id=(ring, member(half, group, core_at)),
            device_id_type=MESH,
        )

    def second_hop(ch, half, kh, step, back=False):
        there = lax.rem(across[half] + step, 4)
        return pltpu.make_async_remote_copy(
            src_ref=part_buf.at[ch, half, kh, there],
            dst_ref=sum_buf.at[ch, half, kh, there if back else across[half]],
            send_sem=b_send.at[ch, half, kh, step],
            recv_sem=b_recv.at[ch, half, kh, there if back else across[half]],
            device_id=(ring, member(1 - half, there, core)),
            device_id_type=MESH,
        )

    first_order = ((1, 0), (3, 0), (1, 1), (3, 1), (2, 0), (2, 1), (0, 1))

    parts = (pl.ds(0, 64), pl.ds(64, 64), pl.ds(128, 32))

    def send_part(ch, part):
        if part == 2:
            for half in range(2):
                own_copy(ch, half).start()
        for step, flip in first_order:
            for half in range(2):
                first_hop(ch, half, step, flip, rows=parts[part]).start()

    def hop(ch, half, kh, side, s):
        sign = 1 if side == 0 else -1
        return pltpu.make_async_remote_copy(
            src_ref=out_ref.at[4 + sign * (s - 1), ch, half, kh],
            dst_ref=out_ref.at[4 + sign * s, ch, half, kh],
            send_sem=z_send.at[ch, half, kh, side, s],
            recv_sem=z_recv.at[ch, half, kh, side, s],
            device_id=(below if side == 0 else above, me),
            device_id_type=MESH,
        )

    def hops_of(ch, side):
        return 4 if ch == side else 3

    def relay(ch, half, kh, s):
        for side in range(2):
            if 2 <= s <= hops_of(ch, side) + 1:
                hop(ch, half, kh, side, s - 1).wait_recv()
            if s <= hops_of(ch, side):
                hop(ch, half, kh, side, s).start()

    def relays(ch, s):
        for kh in range(2):
            for half in range(2):
                relay(ch, half, kh, s)

    def collect(ch, half):
        own_copy(ch, half).wait()
        for step, flip in first_order:
            first_hop(ch, half, step, flip, back=True).wait_recv()
        for s in range(2):
            for o in range(2):
                cols = pl.ds(128 * o, 128)
                for c in range(2):
                    high, low = split(recv_buf[ch, half, 4 * s + 2 * o + c])
                    v_cat[half, s, pl.ds(3 * c * ROWS, ROWS), cols] = high
                    v_cat[half, s, pl.ds((3 * c + 1) * ROWS, ROWS), cols] = low
                    v_cat[half, s, pl.ds((3 * c + 2) * ROWS, ROWS), cols] = high

    def axial(ch, half, kh):
        for s in range(2):
            q_buf[s] = jnp.dot(axial_ref[kh], v_cat[half, s], preferred_element_type=f32)

        k = lax.broadcasted_iota(jnp.int32, (16, 256), 0)
        o = lax.broadcasted_iota(jnp.int32, (16, 256), 1) // 128
        scale = 1.0 / math.sqrt(NX * NZ)
        cos_of, sin_of = [], []
        for s in range(2):
            group = 2 * s + o
            steps = 4 * x_at + group if half == 0 else 4 * group + y_at
            psi = lax.rem(k * steps, 16).astype(f32) * (2.0 * math.pi / 16)
            cos_of.append(jnp.cos(psi) * scale)
            sin_of.append(jnp.sin(psi) * scale)
        lane = lax.broadcasted_iota(jnp.int32, (16, 128), 1)
        even = lane % 2 == 0
        mine = 8 * half + place[half] * 2 + core
        shift = lax.rem(128 - 8 * mine, 128)
        for blk in range(KX // 32):
            p = q = 0.0
            for s in range(2):
                a = q_buf[s, pl.ds(16 * blk, 16), :]
                b = q_buf[s, pl.ds(KX // 2 + 16 * blk, 16), :]
                p = p + (a * cos_of[s] - b * sin_of[s])
                q = q + (a * sin_of[s] + b * cos_of[s])
            p = p[:, :128] + p[:, 128:]
            q = q[:, :128] + q[:, 128:]
            q = jnp.where(even, -q, q)
            turn_buf[0, pl.ds(16 * blk, 16), :] = lane_roll(p, shift)
            turn_buf[1, pl.ds(16 * blk, 16), :] = lane_roll(q, shift)
        for blk in range(2):
            rows = pl.ds(128 * blk, 128)
            for which in range(2):
                flip_buf[which, blk] = turn_buf[which, rows, :].T
            for there in range(4):
                for ri in range(2):
                    straight = flip_buf[0, blk, pl.ds(2 * there + ri, 16, stride=8), :]
                    crossed = flip_buf[1, blk, pl.ds(2 * there + 1 - ri, 16, stride=8), :]
                    part_buf[ch, half, kh, there, ri, :, rows] = straight + crossed
        for step in (1, 3, 2):
            second_hop(ch, half, kh, step).start()

    def gather(ch, half, kh):
        total = part_buf[ch, half, kh, across[half]]
        for step in (1, 3, 2):
            second_hop(ch, half, kh, step, back=True).wait_recv()
        for step in range(1, 4):
            total = total + sum_buf[ch, half, kh, lax.rem(across[half] + step, 4)]
        out_ref[4, ch, half, kh] = total
        relay(ch, half, kh, 1)

    def body(q, _):
        @pl.when(q < groups // 2)
        def _():
            for s in range(2):
                load(s, q).wait()

        for odd in range(2):
            regroup(2 * q + odd - 2, (z_even, z_odd)[odd])
            if odd == 0:
                products(hi_odd, lo_odd, z_odd)
                residues(2 * q, hi_even, lo_even)
            else:
                products(hi_even, lo_even, z_even)
                residues(2 * q + 1, hi_odd, lo_odd)

        @pl.when(q == 2)
        def _():
            pl.semaphore_wait(barrier, 15)
            send_part(0, 0)

        for at, ch, part in ((4, 0, 1), (5, 0, 2), (7, 1, 0)):

            @pl.when(q == at)
            def _():
                send_part(ch, part)

        return 0

    lax.fori_loop(0, groups, body, 0)
    regroup(2 * groups - 2, z_even)
    products(hi_odd, lo_odd, z_odd)
    regroup(2 * groups - 1, z_odd)
    tables_in.wait()
    collect(0, 0)
    axial(0, 0, 0)
    collect(0, 1)
    axial(0, 1, 0)
    send_part(1, 1)
    axial(0, 0, 1)
    axial(0, 1, 1)
    send_part(1, 2)
    for kh in range(2):
        for half in range(2):
            gather(0, half, kh)
    relays(0, 2)
    collect(1, 0)
    axial(1, 0, 0)
    collect(1, 1)
    axial(1, 1, 0)
    relays(0, 3)
    axial(1, 0, 1)
    axial(1, 1, 1)
    for kh in range(2):
        for half in range(2):
            gather(1, half, kh)
    relays(0, 4)
    relays(1, 2)
    relays(0, 5)
    for s in range(3, 6):
        relays(1, s)
    for ch in range(2):
        for half in range(2):
            for step, flip in first_order:
                first_hop(ch, half, step, flip).wait_send()
            for kh in range(2):
                for step in (1, 3, 2):
                    second_hop(ch, half, kh, step).wait_send()
                for side in range(2):
                    for s in range(1, hops_of(ch, side) + 1):
                        hop(ch, half, kh, side, s).wait_send()


def cross_kernel(flag_ref, spec_ref, band_ref, partner_ref):
    ring = lax.axis_index("plane")
    own = pl.program_id(0)
    for i in range(2):

        @pl.when(own == i)
        def _():
            def pair(g, _):
                half = g // 2
                row = pl.multiple_of(lax.rem(g, 2) * 8, 8)
                at = pl.multiple_of(g * 8, 8)
                for kh in range(2):
                    cols = pl.ds(KX // 2 * kh, KX // 2)
                    re0 = spec_ref[4, i, half, kh, 0, pl.ds(row, 8), :]
                    im0 = spec_ref[4, i, half, kh, 1, pl.ds(row, 8), :]
                    for which, out, sign in ((0, band_ref, 1), (1, partner_ref, -1)):
                        for d in range(BAND):
                            off, odd = divmod(i + sign * d, 2)
                            re1 = spec_ref[4 + off, odd, half, kh, 0, pl.ds(row, 8), :]
                            im1 = spec_ref[4 + off, odd, half, kh, 1, pl.ds(row, 8), :]
                            ask = flag_ref[which, i * BAND + d] != 0
                            re, im = re0 * re1 + im0 * im1, im0 * re1 - re0 * im1
                            out[0, d, 0, pl.ds(at, 8), cols] = jnp.where(ask, re, 0.0)
                            out[0, d, 1, pl.ds(at, 8), cols] = jnp.where(ask, im, 0.0)
                return 0

            lax.fori_loop(0, 4, pair, 0)


def local(velocity, plane_slot, pair_list):
    span, twist, axial_cat = [jnp.asarray(t) for t in tables()]
    vmem = pl.BlockSpec(memory_space=pltpu.VMEM)
    hbm = pl.BlockSpec(memory_space=pltpu.HBM)
    slab = (2, 2, 2, 2, 16, KX // 2)
    dma = pltpu.SemaphoreType.DMA
    spectra = pl.pallas_call(
        transform_kernel,
        out_shape=jax.ShapeDtypeStruct((9,) + slab, f32),
        in_specs=[pl.BlockSpec(memory_space=pltpu.SMEM), hbm, vmem, vmem, hbm],
        out_specs=vmem,
        scratch_shapes=[
            pltpu.VMEM((2, ROWS, NZ), f32),
            pltpu.VMEM((2, KX, DEPTH), bf16),
            pltpu.VMEM((2, 8, 16, 512), bf16),
            pltpu.VMEM((2, 8, 16, 512), bf16),
            pltpu.VMEM((2, 8, 16, 512), bf16),
            pltpu.VMEM((2, 8, 16, 512), bf16),
            pltpu.VMEM((2, 8, 16, 128), f32),
            pltpu.VMEM((2, 8, 16, 128), f32),
            pltpu.VMEM((2, CLASSES, ROWS, 128), f32),
            pltpu.VMEM((2, 2, 8, ROWS, 128), f32),
            pltpu.VMEM((2, 2, DEPTH, 256), bf16),
            pltpu.VMEM((2, KX, 256), f32),
            pltpu.VMEM((2, KX // 2, 128), f32),
            pltpu.VMEM((2, 2, 128, 128), f32),
            pltpu.VMEM((2, 2, 2, 4, 2, 16, KX // 2), f32),
            pltpu.VMEM((2, 2, 2, 4, 2, 16, KX // 2), f32),
            dma((2, ROWS // 32)),
            dma,
            dma((2, 2)),
            dma((2, 2, 8)),
            dma((2, 2, 8)),
            dma((2, 2, 2, 4)),
            dma((2, 2, 2, 4)),
            dma((2, 2, 2, 2, 5)),
            dma((2, 2, 2, 2, 5)),
        ],
        compiler_params=pltpu.CompilerParams(
            collective_id=0, has_side_effects=True, vmem_limit_bytes=40 * 1024 * 1024
        ),
        name="transform",
    )(plane_slot, pltpu.with_memory_space_constraint(velocity, pltpu.HBM), span, twist, pltpu.with_memory_space_constraint(axial_cat, pltpu.HBM))

    first_plane = lax.axis_index("plane") * 2
    code = pair_list[:, 0] * BAND + pair_list[:, 1] - pair_list[:, 0]
    own = first_plane + lax.broadcasted_iota(jnp.int32, (2, BAND), 0)
    gap = lax.broadcasted_iota(jnp.int32, (2, BAND), 1)
    up = own * BAND + gap
    down = jnp.where(own >= gap, (own - gap) * BAND + gap, -1)
    asked = jnp.stack([up, down]).reshape(2, 2 * BAND, 1)
    flags = jnp.any(asked == code, axis=2).astype(jnp.int32)

    share = KZ // PEERS
    out = jax.ShapeDtypeStruct((2, BAND, 2, share, KX), f32)
    block = pl.BlockSpec((1, BAND, 2, share, KX), lambda i: (i, 0, 0, 0, 0))
    band_cross, partner_cross = pl.pallas_call(
        cross_kernel,
        grid=(2,),
        out_shape=(out, out),
        in_specs=[
            pl.BlockSpec(memory_space=pltpu.SMEM),
            vmem,
        ],
        out_specs=(block, block),
        compiler_params=pltpu.CompilerParams(vmem_limit_bytes=24 * 1024 * 1024),
        name="cross",
    )(flags, spectra)
    return (band_cross, partner_cross)


def solution(mesh):
    return jax.shard_map(
        local,
        mesh=mesh,
        in_specs=(P("plane", "pencil", None), P(), P()),
        out_specs=(P("plane", None, None, "pencil", None), P("plane", None, None, "pencil", None)),
        check_vma=False,
    )
```

```python
import functools
import math

import jax
import jax.numpy as jnp
import numpy as np
from jax import lax
from jax.experimental import pallas as pl
from jax.experimental.pallas import tpu as pltpu
from jax.sharding import PartitionSpec as P

NX = 5120
NZ = 3840
KX = 512
KZ = 1024
BAND = 8
CLASSES = 16
SPAN = NZ // CLASSES
PEERS = 32
RINGS = 8
ROWS = NX // PEERS
DEPTH = 1024
MESH = pl.DeviceIdType.MESH
bf16 = jnp.bfloat16
f32 = jnp.float32


def split_np(table):
    high = np.asarray(table, np.float32).astype(bf16)
    low = (table - high.astype(np.float64)).astype(np.float32).astype(bf16)
    return high, low


@functools.cache
def tables():
    lane = np.arange(128)
    route, other, ri = lane // 8, lane // 2 % 4, lane % 2
    first, group, core = route // 8, route // 2 % 4, route % 2
    x_at = np.where(first == 0, other, group)
    y_at = np.where(first == 0, group, other)
    m = 2 * (x_at * 8 + y_at * 2 + core) + first
    z = np.arange(256)
    phase = 2 * np.pi * ((z[:, None] * m[None, :]) % SPAN) / SPAN
    real_rows = np.where(ri == 0, np.cos(phase), -np.sin(phase))
    imag_rows = np.where(ri == 0, np.sin(phase), np.cos(phase))
    inside = (z < SPAN)[:, None]
    span = np.concatenate([real_rows * inside, imag_rows * inside], axis=0)

    c = np.arange(CLASSES)
    turn = 2 * np.pi * (c[:, None] * z[None, :]) / NZ
    keep = (z < SPAN)[None, :]
    twist = np.stack([np.cos(turn) * keep, np.sin(turn) * keep], axis=1).astype(np.float32)

    k = np.arange(KX)
    kx = np.where(k < KX // 2, k, k - KX)
    r = np.arange(2 * ROWS)
    theta = 2 * np.pi * ((kx[:, None] * r[None, :]) % NX) / NX
    ax_hi, ax_lo = split_np(np.concatenate([np.cos(theta), np.sin(theta)], axis=0))
    parts = []
    for core in range(2):
        rows = slice(core * ROWS, core * ROWS + ROWS)
        parts += [ax_hi[:, rows], ax_hi[:, rows], ax_lo[:, rows]]
    parts.append(np.zeros((2 * KX, DEPTH - 6 * ROWS), bf16))
    axial = np.concatenate(parts, axis=1).reshape(2, 2, KX // 2, DEPTH)
    axial = np.ascontiguousarray(axial.transpose(1, 0, 2, 3)).reshape(2, KX, DEPTH)
    return np.stack(split_np(span)), twist, axial


def times(a, w):
    ar, ai = a
    wr, wi = w
    s = math.sqrt(0.5)
    if abs(wr - 1) < 1e-12:
        return a
    if abs(wr) < 1e-12 and abs(wi + 1) < 1e-12:
        return (ai, None if ar is None else -ar)
    if abs(wr - s) < 1e-12 and abs(wi + s) < 1e-12 and ai is not None:
        return ((ar + ai) * s, (ai - ar) * s)
    if ai is None:
        return (ar * wr, ar * wi)
    return (ar * wr - ai * wi, ar * wi + ai * wr)


def add(a, b):
    if a is None:
        return b
    if b is None:
        return a
    return a + b


def sub(a, b):
    if b is None:
        return a
    if a is None:
        return -b
    return a - b


def real_fft(xs):
    n = len(xs)
    if n == 1:
        return [(xs[0], None)]
    even = real_fft(xs[0::2])
    odd = real_fft(xs[1::2])
    out = [None] * (n // 2 + 1)
    for k in range(n // 4 + 1):
        w = (math.cos(2 * math.pi * k / n), -math.sin(2 * math.pi * k / n))
        er, ei = even[k]
        tr, ti = times(odd[k], w)
        out[k] = (add(er, tr), add(ei, ti))
        if n // 2 - k != k:
            out[n // 2 - k] = (sub(er, tr), sub(ti, ei))
    return out


def twisted_pair(modes, i, cos_of, sin_of):
    stack = lambda u, v: jnp.concatenate([u, v], axis=0)
    a, b = modes[i]
    if i == 0:
        e = modes[8][0]
        return stack(a, e * cos_of(8)), stack(jnp.zeros_like(a), -(e * sin_of(8)))
    tc, ts = cos_of(i), sin_of(i)
    uc, us = cos_of(16 - i), sin_of(16 - i)
    return stack(a * tc + b * ts, a * uc - b * us), stack(b * tc - a * ts, -(b * uc + a * us))


def split(x):
    high = x.astype(bf16)
    return high, (x - high.astype(f32)).astype(bf16)


def lane_exchange(tiles, lane, roll):
    turned = [t if c == 0 else roll(t, 8 * c) for c, t in enumerate(tiles)]
    tiles = [turned[-j % 16] for j in range(16)]
    for bit in range(4):
        gap = 1 << bit
        high_block = (lane & (8 * gap)) != 0
        tiles = [jnp.where(high_block, tiles[j - gap], tiles[j]) for j in range(16)]
    return tiles


def lane_roll(x, shift):
    return pltpu.roll(x, shift, 1)


def transform_kernel(
    slot_ref, vel_hbm, span_hbm, twist_hbm, axial_hbm, pair_ref, out_ref, flag_ref,
    vel, span_ref, twist_ref, axial_ref, hi_even, lo_even, hi_odd, lo_odd, z_even, z_odd, send_buf, recv_buf, v_cat, q_buf, turn_buf,
    flip_buf, part_buf, sum_buf, load_sem, table_sem, own_sem, a_send, a_recv, b_send, b_recv,
    z_send, z_recv,
):
    me = lax.axis_index("pencil")
    ring = lax.axis_index("plane")
    below = lax.rem(ring + RINGS - 1, RINGS)
    above = lax.rem(ring + 1, RINGS)
    core = lax.rem(me, 2)
    y_at = lax.rem(me // 2, 4)
    x_at = me // 8
    place = (y_at, x_at)
    across = (x_at, y_at)

    def member(half, group, core_at):
        if half == 0:
            return x_at * 8 + group * 2 + core_at
        return group * 8 + y_at * 2 + core_at

    barrier = pltpu.get_barrier_semaphore()

    def load(slot, part):
        rows = pl.ds(part * 32, 32)
        return pltpu.make_async_copy(
            vel_hbm.at[slot, rows], vel.at[slot, rows], load_sem.at[slot, part]
        )

    twist_in = pltpu.make_async_copy(twist_hbm, twist_ref, table_sem.at[0])
    span_in = pltpu.make_async_copy(span_hbm, span_ref, table_sem.at[1])
    tables_in = pltpu.make_async_copy(axial_hbm, axial_ref, table_sem.at[2])
    twist_in.start()
    for part in range(ROWS // 32):
        for slot in range(2):
            load(slot, part).start()
        if part == 0:
            span_in.start()
    tables_in.start()
    for half in range(2):
        for step in range(4):
            for flip in range(2):
                if step == 0 and (flip == 0 or half == 1):
                    continue
                peer = member(half, lax.rem(place[half] + step, 4), lax.rem(core + flip, 2))
                pl.semaphore_signal(barrier, inc=1, device_id=(ring, peer), device_id_type=MESH)
    for other in (below, above):
        pl.semaphore_signal(barrier, inc=1, device_id=(other, me), device_id_type=MESH)
    for half in range(2):
        for s in range(2):
            rest = pl.ds(6 * ROWS, DEPTH - 6 * ROWS)
            v_cat[half, s, rest, :] = jnp.zeros((DEPTH - 6 * ROWS, 256), bf16)

    lane8 = lax.broadcasted_iota(jnp.int32, (8, 128), 1)
    groups = ROWS // 16

    def residues(g, y_hi, y_lo):
        slot = lax.rem(slot_ref[2 * ring + g // groups], 2)
        row = pl.multiple_of(lax.rem(g, groups) * 16, 16)

        def tile(k, half):
            at = (pl.ds(row + 8 * half, 8), pl.ds(128 * (k % 30), 128))
            return jnp.where(slot == 0, vel[(0,) + at], vel[(1,) + at])

        for part, half in ((0, 0), (0, 1), (1, 0), (1, 1)):
            xs = []
            for j in range(CLASSES):
                first, shift = divmod(SPAN * j + 128 * part, 128)
                if shift == 0:
                    xs.append(tile(first, half))
                    continue
                xs.append(
                    jnp.where(
                        lane8 < 128 - shift,
                        lane_roll(tile(first, half), 128 - shift),
                        lane_roll(tile(first + 1, half), 128 - shift),
                    )
                )
            cols = pl.ds(128 * part, 128)
            cos_of = lambda c: jnp.broadcast_to(twist_ref[c, 0:1, cols], (8, 128))
            sin_of = lambda c: jnp.broadcast_to(twist_ref[c, 1:2, cols], (8, 128))
            modes = real_fft(xs)
            for i in range(8):
                for which, value in enumerate(twisted_pair(modes, i, cos_of, sin_of)):
                    at = pl.ds(256 * which + 128 * part, 128)
                    y_hi[half, i, :, at], y_lo[half, i, :, at] = split(value)

    def products(y_hi, y_lo, z_buf):
        high = y_hi[...].reshape(CLASSES * 16, 512)
        low = y_lo[...].reshape(CLASSES * 16, 512)
        total = jnp.dot(high, span_ref[0], preferred_element_type=f32)
        total += jnp.dot(low, span_ref[0], preferred_element_type=f32)
        total += jnp.dot(high, span_ref[1], preferred_element_type=f32)
        z_buf[...] = total.reshape(2, 8, 16, 128)

    def regroup(g, z_buf):
        g = jnp.maximum(g, 0)
        row = pl.multiple_of(lax.rem(g, groups) * 16, 16)
        for part in range(2):
            tiles = [z_buf[part, min(c, 16 - c) % 8, pl.ds(c // 8 * 8, 8), :] for c in range(CLASSES)]
            for f, tile in enumerate(lane_exchange(tiles, lane8, lane_roll)):
                send_buf[g // groups, f, pl.ds(row + 8 * part, 8), :] = tile

    def own_copy(ch, half):
        mine = place[half] * 2 + core
        return pltpu.make_async_copy(
            send_buf.at[ch, 8 * half + mine], recv_buf.at[ch, half, mine], own_sem.at[ch, half]
        )

    def first_hop(ch, half, step, flip, back=False, rows=pl.ds(0, ROWS)):
        mine = place[half] * 2 + core
        group = lax.rem(place[half] + step, 4)
        core_at = lax.rem(core + flip, 2)
        peer = group * 2 + core_at
        return pltpu.make_async_remote_copy(
            src_ref=send_buf.at[ch, 8 * half + peer, rows],
            dst_ref=recv_buf.at[ch, half, peer if back else mine, rows],
            send_sem=a_send.at[ch, half, 2 * step + flip],
            recv_sem=a_recv.at[ch, half, peer if back else mine],
            device_id=(ring, member(half, group, core_at)),
            device_id_type=MESH,
        )

    def second_hop(ch, half, kh, step, back=False):
        there = lax.rem(across[half] + step, 4)
        return pltpu.make_async_remote_copy(
            src_ref=part_buf.at[ch, half, kh, there],
            dst_ref=sum_buf.at[ch, half, kh, there if back else across[half]],
            send_sem=b_send.at[ch, half, kh, step],
            recv_sem=b_recv.at[ch, half, kh, there if back else across[half]],
            device_id=(ring, member(1 - half, there, core)),
            device_id_type=MESH,
        )

    first_order = ((1, 0), (3, 0), (1, 1), (3, 1), (2, 0), (2, 1), (0, 1))

    parts = (pl.ds(0, 64), pl.ds(64, 64), pl.ds(128, 32))

    def send_part(ch, part):
        if part == 2:
            for half in range(2):
                own_copy(ch, half).start()
        for step, flip in first_order:
            for half in range(2):
                first_hop(ch, half, step, flip, rows=parts[part]).start()

    def hop(ch, half, kh, side, s):
        sign = 1 if side == 0 else -1
        return pltpu.make_async_remote_copy(
            src_ref=out_ref.at[4 + sign * (s - 1), ch, half, kh],
            dst_ref=out_ref.at[4 + sign * s, ch, half, kh],
            send_sem=z_send.at[ch, half, kh, side, s],
            recv_sem=z_recv.at[ch, half, kh, side, s],
            device_id=(below if side == 0 else above, me),
            device_id_type=MESH,
        )

    def hops_of(ch, side):
        return 4 if ch == side else 3

    def relay(ch, half, kh, s):
        for side in range(2):
            if s > hops_of(ch, side):
                continue
            if s > 1:
                hop(ch, half, kh, side, s - 1).wait_recv()
            hop(ch, half, kh, side, s).start()

    def relays(ch, kh, s):
        for half in range(2):
            relay(ch, half, kh, s)

    def collect(ch, half):
        own_copy(ch, half).wait()
        for step, flip in first_order:
            first_hop(ch, half, step, flip, back=True).wait_recv()
        for s in range(2):
            for o in range(2):
                cols = pl.ds(128 * o, 128)
                for c in range(2):
                    high, low = split(recv_buf[ch, half, 4 * s + 2 * o + c])
                    v_cat[half, s, pl.ds(3 * c * ROWS, ROWS), cols] = high
                    v_cat[half, s, pl.ds((3 * c + 1) * ROWS, ROWS), cols] = low
                    v_cat[half, s, pl.ds((3 * c + 2) * ROWS, ROWS), cols] = high

    def axial(ch, half, kh):
        for s in range(2):
            q_buf[s] = jnp.dot(axial_ref[kh], v_cat[half, s], preferred_element_type=f32)

        k = lax.broadcasted_iota(jnp.int32, (16, 256), 0)
        o = lax.broadcasted_iota(jnp.int32, (16, 256), 1) // 128
        scale = 1.0 / math.sqrt(NX * NZ)
        cos_of, sin_of = [], []
        for s in range(2):
            group = 2 * s + o
            steps = 4 * x_at + group if half == 0 else 4 * group + y_at
            psi = lax.rem(k * steps, 16).astype(f32) * (2.0 * math.pi / 16)
            cos_of.append(jnp.cos(psi) * scale)
            sin_of.append(jnp.sin(psi) * scale)
        lane = lax.broadcasted_iota(jnp.int32, (16, 128), 1)
        even = lane % 2 == 0
        mine = 8 * half + place[half] * 2 + core
        shift = lax.rem(128 - 8 * mine, 128)
        for blk in range(KX // 32):
            p = q = 0.0
            for s in range(2):
                a = q_buf[s, pl.ds(16 * blk, 16), :]
                b = q_buf[s, pl.ds(KX // 2 + 16 * blk, 16), :]
                p = p + (a * cos_of[s] - b * sin_of[s])
                q = q + (a * sin_of[s] + b * cos_of[s])
            p = p[:, :128] + p[:, 128:]
            q = q[:, :128] + q[:, 128:]
            q = jnp.where(even, -q, q)
            turn_buf[0, pl.ds(16 * blk, 16), :] = lane_roll(p, shift)
            turn_buf[1, pl.ds(16 * blk, 16), :] = lane_roll(q, shift)
        for blk in range(2):
            rows = pl.ds(128 * blk, 128)
            for which in range(2):
                flip_buf[which, blk] = turn_buf[which, rows, :].T
            for there in range(4):
                for ri in range(2):
                    straight = flip_buf[0, blk, pl.ds(2 * there + ri, 16, stride=8), :]
                    crossed = flip_buf[1, blk, pl.ds(2 * there + 1 - ri, 16, stride=8), :]
                    part_buf[ch, half, kh, there, ri, :, rows] = straight + crossed
        for step in (1, 3, 2):
            second_hop(ch, half, kh, step).start()

    def gather(ch, half, kh):
        total = part_buf[ch, half, kh, across[half]]
        for step in (1, 3, 2):
            second_hop(ch, half, kh, step, back=True).wait_recv()
        for step in range(1, 4):
            total = total + sum_buf[ch, half, kh, lax.rem(across[half] + step, 4)]
        out_ref[4, ch, half, kh] = total
        relay(ch, half, kh, 1)

    def body(q, _):
        @pl.when(q < groups // 2)
        def _():
            for s in range(2):
                load(s, q).wait()

        for odd in range(2):
            regroup(2 * q + odd - 2, (z_even, z_odd)[odd])
            if odd == 0:
                products(hi_odd, lo_odd, z_odd)
                residues(2 * q, hi_even, lo_even)
            else:
                products(hi_even, lo_even, z_even)
                residues(2 * q + 1, hi_odd, lo_odd)

        @pl.when(q == 2)
        def _():
            pl.semaphore_wait(barrier, 15)
            send_part(0, 0)

        for at, ch, part in ((4, 0, 1), (5, 0, 2), (7, 1, 0)):

            @pl.when(q == at)
            def _():
                send_part(ch, part)

        return 0

    twist_in.wait()
    span_in.wait()
    lax.fori_loop(0, groups, body, 0)
    regroup(2 * groups - 2, z_even)
    products(hi_odd, lo_odd, z_odd)
    regroup(2 * groups - 1, z_odd)
    index = lax.broadcasted_iota(jnp.int32, (1, 128), 1)
    own_plane = 2 * ring + index // BAND % 2
    gap = index % BAND
    code = jnp.where(index < 2 * BAND, own_plane, own_plane - gap) * BAND + gap
    lower = pair_ref[:, 0:1]
    asked = lower * BAND + pair_ref[:, 1:2] - lower == code
    asked = jnp.max(asked.astype(jnp.int32), axis=0, keepdims=True)
    flag_ref[...] = jnp.where(own_plane - gap < 0, jnp.where(index < 2 * BAND, asked, 0), asked)
    tables_in.wait()
    collect(0, 0)
    axial(0, 0, 0)
    collect(0, 1)
    axial(0, 1, 0)
    send_part(1, 1)
    axial(0, 0, 1)
    send_part(1, 2)
    axial(0, 1, 1)
    for kh in range(2):
        for half in range(2):
            gather(0, half, kh)
    for kh in range(2):
        relays(0, kh, 2)
    collect(1, 0)
    axial(1, 0, 0)
    relays(0, 0, 3)
    collect(1, 1)
    axial(1, 1, 0)
    relays(0, 1, 3)
    axial(1, 0, 1)
    axial(1, 1, 1)
    relays(0, 0, 4)
    for half in range(2):
        gather(1, half, 0)
    relays(0, 1, 4)
    for half in range(2):
        gather(1, half, 1)
    for s in range(2, 5):
        for kh in range(2):
            relays(1, kh, s)
    for ch in range(2):
        for half in range(2):
            for step, flip in first_order:
                first_hop(ch, half, step, flip).wait_send()
            for kh in range(2):
                for step in (1, 3, 2):
                    second_hop(ch, half, kh, step).wait_send()
                for side in range(2):
                    hop(ch, half, kh, side, hops_of(ch, side)).wait_recv()
                    for s in range(1, hops_of(ch, side) + 1):
                        hop(ch, half, kh, side, s).wait_send()


def cross_kernel(flag_ref, spec_ref, band_ref, partner_ref):
    own = pl.program_id(0)
    half = pl.program_id(1)
    for i in range(2):

        @pl.when(own == i)
        def _():
            def pair(g, _):
                row = pl.multiple_of(g * 8, 8)
                for kh in range(2):
                    cols = pl.ds(KX // 2 * kh, KX // 2)
                    re0 = spec_ref[4, i, half, kh, 0, pl.ds(row, 8), :]
                    im0 = spec_ref[4, i, half, kh, 1, pl.ds(row, 8), :]
                    for which, out, sign in ((0, band_ref, 1), (1, partner_ref, -1)):
                        for d in range(BAND):
                            off, odd = divmod(i + sign * d, 2)
                            re1 = spec_ref[4 + off, odd, half, kh, 0, pl.ds(row, 8), :]
                            im1 = spec_ref[4 + off, odd, half, kh, 1, pl.ds(row, 8), :]
                            ask = flag_ref[0, (2 * which + i) * BAND + d] != 0
                            re, im = re0 * re1 + im0 * im1, im0 * re1 - re0 * im1
                            out[0, d, 0, pl.ds(row, 8), cols] = jnp.where(ask, re, 0.0)
                            out[0, d, 1, pl.ds(row, 8), cols] = jnp.where(ask, im, 0.0)
                return 0

            lax.fori_loop(0, 2, pair, 0)


def local(velocity, plane_slot, pair_list):
    span, twist, axial_cat = [jnp.asarray(t) for t in tables()]
    vmem = pl.BlockSpec(memory_space=pltpu.VMEM)
    hbm = pl.BlockSpec(memory_space=pltpu.HBM)
    slab = (2, 2, 2, 2, 16, KX // 2)
    dma = pltpu.SemaphoreType.DMA
    spectra, flags = pl.pallas_call(
        transform_kernel,
        out_shape=(
            jax.ShapeDtypeStruct((9,) + slab, f32),
            jax.ShapeDtypeStruct((1, 128), jnp.int32),
        ),
        in_specs=[pl.BlockSpec(memory_space=pltpu.SMEM), hbm, hbm, hbm, hbm, vmem],
        out_specs=(vmem, vmem),
        scratch_shapes=[
            pltpu.VMEM((2, ROWS, NZ), f32),
            pltpu.VMEM((2, 512, 128), bf16),
            pltpu.VMEM((CLASSES, 2, 256), f32),
            pltpu.VMEM((2, KX, DEPTH), bf16),
            pltpu.VMEM((2, 8, 16, 512), bf16),
            pltpu.VMEM((2, 8, 16, 512), bf16),
            pltpu.VMEM((2, 8, 16, 512), bf16),
            pltpu.VMEM((2, 8, 16, 512), bf16),
            pltpu.VMEM((2, 8, 16, 128), f32),
            pltpu.VMEM((2, 8, 16, 128), f32),
            pltpu.VMEM((2, CLASSES, ROWS, 128), f32),
            pltpu.VMEM((2, 2, 8, ROWS, 128), f32),
            pltpu.VMEM((2, 2, DEPTH, 256), bf16),
            pltpu.VMEM((2, KX, 256), f32),
            pltpu.VMEM((2, KX // 2, 128), f32),
            pltpu.VMEM((2, 2, 128, 128), f32),
            pltpu.VMEM((2, 2, 2, 4, 2, 16, KX // 2), f32),
            pltpu.VMEM((2, 2, 2, 4, 2, 16, KX // 2), f32),
            dma((2, ROWS // 32)),
            dma((3,)),
            dma((2, 2)),
            dma((2, 2, 8)),
            dma((2, 2, 8)),
            dma((2, 2, 2, 4)),
            dma((2, 2, 2, 4)),
            dma((2, 2, 2, 2, 5)),
            dma((2, 2, 2, 2, 5)),
        ],
        compiler_params=pltpu.CompilerParams(
            collective_id=0, has_side_effects=True, vmem_limit_bytes=40 * 1024 * 1024
        ),
        name="transform",
    )(*[
        pltpu.with_memory_space_constraint(array, pltpu.HBM)
        for array in (plane_slot, velocity, span, twist, axial_cat, pair_list)
    ])

    share = KZ // PEERS
    out = jax.ShapeDtypeStruct((2, BAND, 2, share, KX), f32)
    block = pl.BlockSpec((1, BAND, 2, share // 2, KX), lambda i, h: (i, 0, 0, h, 0))
    band_cross, partner_cross = pl.pallas_call(
        cross_kernel,
        grid=(2, 2),
        out_shape=(out, out),
        in_specs=[
            pl.BlockSpec(memory_space=pltpu.SMEM),
            vmem,
        ],
        out_specs=(block, block),
        compiler_params=pltpu.CompilerParams(vmem_limit_bytes=24 * 1024 * 1024),
        name="cross",
    )(flags, spectra)
    return (band_cross, partner_cross)


def solution(mesh):
    return jax.shard_map(
        local,
        mesh=mesh,
        in_specs=(P("plane", "pencil", None), P(), P()),
        out_specs=(P("plane", None, None, "pencil", None), P("plane", None, None, "pencil", None)),
        check_vma=False,
    )
```

```python
import functools
import math

import jax
import jax.numpy as jnp
import numpy as np
from jax import lax
from jax.experimental import pallas as pl
from jax.experimental.pallas import tpu as pltpu
from jax.sharding import PartitionSpec as P

NX = 5120
NZ = 3840
KX = 512
KZ = 1024
BAND = 8
CLASSES = 16
SPAN = NZ // CLASSES
PEERS = 32
RINGS = 8
ROWS = NX // PEERS
DEPTH = 1024
MESH = pl.DeviceIdType.MESH
bf16 = jnp.bfloat16
f32 = jnp.float32


def split_np(table):
    high = np.asarray(table, np.float32).astype(bf16)
    low = (table - high.astype(np.float64)).astype(np.float32).astype(bf16)
    return high, low


@functools.cache
def tables():
    lane = np.arange(128)
    route, other, ri = lane // 8, lane // 2 % 4, lane % 2
    first, group, core = route // 8, route // 2 % 4, route % 2
    x_at = np.where(first == 0, other, group)
    y_at = np.where(first == 0, group, other)
    m = 2 * (x_at * 8 + y_at * 2 + core) + first
    z = np.arange(256)
    phase = 2 * np.pi * ((z[:, None] * m[None, :]) % SPAN) / SPAN
    real_rows = np.where(ri == 0, np.cos(phase), -np.sin(phase))
    imag_rows = np.where(ri == 0, np.sin(phase), np.cos(phase))
    inside = (z < SPAN)[:, None]
    span = np.concatenate([real_rows * inside, imag_rows * inside], axis=0)

    c = np.arange(CLASSES)
    turn = 2 * np.pi * (c[:, None] * z[None, :]) / NZ
    keep = (z < SPAN)[None, :]
    twist = np.stack([np.cos(turn) * keep, np.sin(turn) * keep], axis=1).astype(np.float32)

    k = np.arange(KX)
    kx = np.where(k < KX // 2, k, k - KX)
    r = np.arange(2 * ROWS)
    theta = 2 * np.pi * ((kx[:, None] * r[None, :]) % NX) / NX
    ax_hi, ax_lo = split_np(np.concatenate([np.cos(theta), np.sin(theta)], axis=0))
    parts = []
    for core in range(2):
        rows = slice(core * ROWS, core * ROWS + ROWS)
        parts += [ax_hi[:, rows], ax_hi[:, rows], ax_lo[:, rows]]
    parts.append(np.zeros((2 * KX, DEPTH - 6 * ROWS), bf16))
    axial = np.concatenate(parts, axis=1).reshape(2, 2, KX // 2, DEPTH)
    axial = np.ascontiguousarray(axial.transpose(1, 0, 2, 3)).reshape(2, KX, DEPTH)
    return np.concatenate(split_np(span), axis=1), twist, axial


def times(a, w):
    ar, ai = a
    wr, wi = w
    s = math.sqrt(0.5)
    if abs(wr - 1) < 1e-12:
        return a
    if abs(wr) < 1e-12 and abs(wi + 1) < 1e-12:
        return (ai, None if ar is None else -ar)
    if abs(wr - s) < 1e-12 and abs(wi + s) < 1e-12 and ai is not None:
        return ((ar + ai) * s, (ai - ar) * s)
    if ai is None:
        return (ar * wr, ar * wi)
    return (ar * wr - ai * wi, ar * wi + ai * wr)


def add(a, b):
    if a is None:
        return b
    if b is None:
        return a
    return a + b


def sub(a, b):
    if b is None:
        return a
    if a is None:
        return -b
    return a - b


def real_fft(xs):
    n = len(xs)
    if n == 1:
        return [(xs[0], None)]
    even = real_fft(xs[0::2])
    odd = real_fft(xs[1::2])
    out = [None] * (n // 2 + 1)
    for k in range(n // 4 + 1):
        w = (math.cos(2 * math.pi * k / n), -math.sin(2 * math.pi * k / n))
        er, ei = even[k]
        tr, ti = times(odd[k], w)
        out[k] = (add(er, tr), add(ei, ti))
        if n // 2 - k != k:
            out[n // 2 - k] = (sub(er, tr), sub(ti, ei))
    return out


def twisted_pair(modes, i, cos_of, sin_of):
    stack = lambda u, v: jnp.concatenate([u, v], axis=0)
    a, b = modes[i]
    if i == 0:
        e = modes[8][0]
        return stack(a, e * cos_of(8)), stack(jnp.zeros_like(a), -(e * sin_of(8)))
    tc, ts = cos_of(i), sin_of(i)
    uc, us = cos_of(16 - i), sin_of(16 - i)
    return stack(a * tc + b * ts, a * uc - b * us), stack(b * tc - a * ts, -(b * uc + a * us))


def split(x):
    high = x.astype(bf16)
    return high, (x - high.astype(f32)).astype(bf16)


def lane_exchange(tiles, lane, roll):
    turned = [t if c == 0 else roll(t, 8 * c) for c, t in enumerate(tiles)]
    tiles = [turned[-j % 16] for j in range(16)]
    for bit in range(4):
        gap = 1 << bit
        high_block = (lane & (8 * gap)) != 0
        tiles = [jnp.where(high_block, tiles[j - gap], tiles[j]) for j in range(16)]
    return tiles


def lane_roll(x, shift):
    return pltpu.roll(x, shift, 1)


def transform_kernel(
    slot_ref, vel_hbm, span_hbm, twist_hbm, axial_hbm, pair_ref, out_ref, flag_ref,
    vel, span_ref, twist_ref, axial_ref, hi_even, lo_even, hi_odd, lo_odd, z_even, z_odd, send_buf, recv_buf, v_cat, q_buf, turn_buf,
    flip_buf, part_buf, sum_buf, load_sem, table_sem, own_sem, a_send, a_recv, b_send, b_recv,
    z_send, z_recv,
):
    me = lax.axis_index("pencil")
    ring = lax.axis_index("plane")
    below = lax.rem(ring + RINGS - 1, RINGS)
    above = lax.rem(ring + 1, RINGS)
    core = lax.rem(me, 2)
    y_at = lax.rem(me // 2, 4)
    x_at = me // 8
    place = (y_at, x_at)
    across = (x_at, y_at)

    def member(half, group, core_at):
        if half == 0:
            return x_at * 8 + group * 2 + core_at
        return group * 8 + y_at * 2 + core_at

    barrier = pltpu.get_barrier_semaphore()

    def load(slot, part):
        rows = pl.ds(part * 32, 32)
        return pltpu.make_async_copy(
            vel_hbm.at[slot, rows], vel.at[slot, rows], load_sem.at[slot, part]
        )

    twist_in = pltpu.make_async_copy(twist_hbm, twist_ref, table_sem.at[0])
    span_in = pltpu.make_async_copy(span_hbm, span_ref, table_sem.at[1])
    tables_in = pltpu.make_async_copy(axial_hbm, axial_ref, table_sem.at[2])
    twist_in.start()
    for part in range(ROWS // 32):
        for slot in range(2):
            load(slot, part).start()
        if part == 0:
            span_in.start()
    tables_in.start()
    for half in range(2):
        for step in range(4):
            for flip in range(2):
                if step == 0 and (flip == 0 or half == 1):
                    continue
                peer = member(half, lax.rem(place[half] + step, 4), lax.rem(core + flip, 2))
                pl.semaphore_signal(barrier, inc=1, device_id=(ring, peer), device_id_type=MESH)
    for other in (below, above):
        pl.semaphore_signal(barrier, inc=1, device_id=(other, me), device_id_type=MESH)
    for half in range(2):
        for s in range(2):
            rest = pl.ds(6 * ROWS, DEPTH - 6 * ROWS)
            v_cat[half, s, rest, :] = jnp.zeros((DEPTH - 6 * ROWS, 256), bf16)

    lane8 = lax.broadcasted_iota(jnp.int32, (8, 128), 1)
    groups = ROWS // 16

    def residues(g, y_hi, y_lo):
        slot = lax.rem(slot_ref[2 * ring + g // groups], 2)
        row = pl.multiple_of(lax.rem(g, groups) * 16, 16)

        def tile(k, half):
            at = (pl.ds(row + 8 * half, 8), pl.ds(128 * (k % 30), 128))
            return jnp.where(slot == 0, vel[(0,) + at], vel[(1,) + at])

        for part, half in ((0, 0), (0, 1), (1, 0), (1, 1)):
            xs = []
            for j in range(CLASSES):
                first, shift = divmod(SPAN * j + 128 * part, 128)
                if shift == 0:
                    xs.append(tile(first, half))
                    continue
                xs.append(
                    jnp.where(
                        lane8 < 128 - shift,
                        lane_roll(tile(first, half), 128 - shift),
                        lane_roll(tile(first + 1, half), 128 - shift),
                    )
                )
            cols = pl.ds(128 * part, 128)
            cos_of = lambda c: jnp.broadcast_to(twist_ref[c, 0:1, cols], (8, 128))
            sin_of = lambda c: jnp.broadcast_to(twist_ref[c, 1:2, cols], (8, 128))
            modes = real_fft(xs)
            for i in range(8):
                for which, value in enumerate(twisted_pair(modes, i, cos_of, sin_of)):
                    at = pl.ds(256 * which + 128 * part, 128)
                    y_hi[half, i, :, at], y_lo[half, i, :, at] = split(value)

    def products(y_hi, y_lo, z_buf):
        high = y_hi[...].reshape(CLASSES * 16, 512)
        low = y_lo[...].reshape(CLASSES * 16, 512)
        both = jnp.dot(high, span_ref[...], preferred_element_type=f32)
        total = both[:, :128] + both[:, 128:]
        total += jnp.dot(low, span_ref[:, pl.ds(0, 128)], preferred_element_type=f32)
        z_buf[...] = total.reshape(2, 8, 16, 128)

    def regroup(g, z_buf):
        g = jnp.maximum(g, 0)
        row = pl.multiple_of(lax.rem(g, groups) * 16, 16)
        for part in range(2):
            tiles = [z_buf[part, min(c, 16 - c) % 8, pl.ds(c // 8 * 8, 8), :] for c in range(CLASSES)]
            for f, tile in enumerate(lane_exchange(tiles, lane8, lane_roll)):
                send_buf[g // groups, f, pl.ds(row + 8 * part, 8), :] = tile

    def own_copy(ch, half):
        mine = place[half] * 2 + core
        return pltpu.make_async_copy(
            send_buf.at[ch, 8 * half + mine], recv_buf.at[ch, half, mine], own_sem.at[ch, half]
        )

    def first_hop(ch, half, step, flip, back=False, rows=pl.ds(0, ROWS)):
        mine = place[half] * 2 + core
        group = lax.rem(place[half] + step, 4)
        core_at = lax.rem(core + flip, 2)
        peer = group * 2 + core_at
        return pltpu.make_async_remote_copy(
            src_ref=send_buf.at[ch, 8 * half + peer, rows],
            dst_ref=recv_buf.at[ch, half, peer if back else mine, rows],
            send_sem=a_send.at[ch, half, 2 * step + flip],
            recv_sem=a_recv.at[ch, half, peer if back else mine],
            device_id=(ring, member(half, group, core_at)),
            device_id_type=MESH,
        )

    def second_hop(ch, half, kh, step, back=False):
        there = lax.rem(across[half] + step, 4)
        return pltpu.make_async_remote_copy(
            src_ref=part_buf.at[ch, half, kh, there],
            dst_ref=sum_buf.at[ch, half, kh, there if back else across[half]],
            send_sem=b_send.at[ch, half, kh, step],
            recv_sem=b_recv.at[ch, half, kh, there if back else across[half]],
            device_id=(ring, member(1 - half, there, core)),
            device_id_type=MESH,
        )

    first_order = ((1, 0), (3, 0), (1, 1), (3, 1), (2, 0), (2, 1), (0, 1))

    parts = (pl.ds(0, 32), pl.ds(32, 64), pl.ds(96, 64))

    def send_part(ch, part):
        if part == 2:
            for half in range(2):
                own_copy(ch, half).start()
        for step, flip in first_order:
            for half in range(2):
                first_hop(ch, half, step, flip, rows=parts[part]).start()

    def hop(ch, half, kh, side, s):
        sign = 1 if side == 0 else -1
        return pltpu.make_async_remote_copy(
            src_ref=out_ref.at[4 + sign * (s - 1), ch, half, kh],
            dst_ref=out_ref.at[4 + sign * s, ch, half, kh],
            send_sem=z_send.at[ch, half, kh, side, s],
            recv_sem=z_recv.at[ch, half, kh, side, s],
            device_id=(below if side == 0 else above, me),
            device_id_type=MESH,
        )

    def hops_of(ch, side):
        return 4 if ch == side else 3

    def relay(ch, half, kh, s):
        for side in range(2):
            if s > hops_of(ch, side):
                continue
            if s > 1:
                hop(ch, half, kh, side, s - 1).wait_recv()
            hop(ch, half, kh, side, s).start()

    def relays(ch, kh, s):
        for half in range(2):
            relay(ch, half, kh, s)

    def collect(ch, half):
        own_copy(ch, half).wait()
        for step, flip in first_order:
            first_hop(ch, half, step, flip, back=True).wait_recv()
        for s in range(2):
            for o in range(2):
                cols = pl.ds(128 * o, 128)
                for c in range(2):
                    high, low = split(recv_buf[ch, half, 4 * s + 2 * o + c])
                    v_cat[half, s, pl.ds(3 * c * ROWS, ROWS), cols] = high
                    v_cat[half, s, pl.ds((3 * c + 1) * ROWS, ROWS), cols] = low
                    v_cat[half, s, pl.ds((3 * c + 2) * ROWS, ROWS), cols] = high

    def axial(ch, half, kh):
        for s in range(2):
            q_buf[s] = jnp.dot(axial_ref[kh], v_cat[half, s], preferred_element_type=f32)

        k = lax.broadcasted_iota(jnp.int32, (16, 256), 0)
        o = lax.broadcasted_iota(jnp.int32, (16, 256), 1) // 128
        scale = 1.0 / math.sqrt(NX * NZ)
        cos_of, sin_of = [], []
        for s in range(2):
            group = 2 * s + o
            steps = 4 * x_at + group if half == 0 else 4 * group + y_at
            psi = lax.rem(k * steps, 16).astype(f32) * (2.0 * math.pi / 16)
            cos_of.append(jnp.cos(psi) * scale)
            sin_of.append(jnp.sin(psi) * scale)
        lane = lax.broadcasted_iota(jnp.int32, (16, 128), 1)
        even = lane % 2 == 0
        mine = 8 * half + place[half] * 2 + core
        shift = lax.rem(128 - 8 * mine, 128)
        for blk in range(KX // 32):
            p = q = 0.0
            for s in range(2):
                a = q_buf[s, pl.ds(16 * blk, 16), :]
                b = q_buf[s, pl.ds(KX // 2 + 16 * blk, 16), :]
                p = p + (a * cos_of[s] - b * sin_of[s])
                q = q + (a * sin_of[s] + b * cos_of[s])
            p = p[:, :128] + p[:, 128:]
            q = q[:, :128] + q[:, 128:]
            q = jnp.where(even, -q, q)
            turn_buf[0, pl.ds(16 * blk, 16), :] = lane_roll(p, shift)
            turn_buf[1, pl.ds(16 * blk, 16), :] = lane_roll(q, shift)
        for blk in range(2):
            rows = pl.ds(128 * blk, 128)
            for which in range(2):
                flip_buf[which, blk] = turn_buf[which, rows, :].T
            for there in range(4):
                for ri in range(2):
                    straight = flip_buf[0, blk, pl.ds(2 * there + ri, 16, stride=8), :]
                    crossed = flip_buf[1, blk, pl.ds(2 * there + 1 - ri, 16, stride=8), :]
                    part_buf[ch, half, kh, there, ri, :, rows] = straight + crossed
        for step in (1, 3, 2):
            second_hop(ch, half, kh, step).start()

    def gather(ch, half, kh):
        total = part_buf[ch, half, kh, across[half]]
        for step in (1, 3, 2):
            second_hop(ch, half, kh, step, back=True).wait_recv()
        for step in range(1, 4):
            total = total + sum_buf[ch, half, kh, lax.rem(across[half] + step, 4)]
        out_ref[4, ch, half, kh] = total
        relay(ch, half, kh, 1)

    def body(q, _):
        @pl.when(q < groups // 2)
        def _():
            for s in range(2):
                load(s, q).wait()

        for odd in range(2):
            regroup(2 * q + odd - 2, (z_even, z_odd)[odd])
            if odd == 0:
                products(hi_odd, lo_odd, z_odd)
                residues(2 * q, hi_even, lo_even)
            else:
                products(hi_even, lo_even, z_even)
                residues(2 * q + 1, hi_odd, lo_odd)

        @pl.when(q == 1)
        def _():
            pl.semaphore_wait(barrier, 15)
            send_part(0, 0)

        for at, ch, part in ((3, 0, 1), (5, 0, 2), (6, 1, 0), (8, 1, 1)):

            @pl.when(q == at)
            def _():
                send_part(ch, part)

        return 0

    twist_in.wait()
    span_in.wait()
    lax.fori_loop(0, groups, body, 0)
    regroup(2 * groups - 2, z_even)
    products(hi_odd, lo_odd, z_odd)
    regroup(2 * groups - 1, z_odd)
    index = lax.broadcasted_iota(jnp.int32, (4 * BAND, 1), 0)
    own_plane = 2 * ring + index // BAND % 2
    gap = index % BAND
    code = jnp.where(index < 2 * BAND, own_plane, own_plane - gap) * BAND + gap
    lower = pair_ref[0:1, :]
    asked = lower * BAND + pair_ref[1:2, :] - lower == code
    asked = jnp.max(jnp.where(asked, 1.0, 0.0), axis=1, keepdims=True)
    asked = jnp.where((index >= 2 * BAND) & (own_plane < gap), 0.0, asked)
    flag_ref[...] = jnp.broadcast_to(asked, (4 * BAND, KX // 2))
    tables_in.wait()
    collect(0, 0)
    axial(0, 0, 0)
    collect(0, 1)
    axial(0, 1, 0)
    send_part(1, 2)
    axial(0, 0, 1)
    axial(0, 1, 1)
    for kh in range(2):
        for half in range(2):
            gather(0, half, kh)
    for kh in range(2):
        relays(0, kh, 2)
    collect(1, 0)
    axial(1, 0, 0)
    relays(0, 0, 3)
    collect(1, 1)
    axial(1, 1, 0)
    relays(0, 1, 3)
    axial(1, 0, 1)
    axial(1, 1, 1)
    relays(0, 0, 4)
    for half in range(2):
        gather(1, half, 0)
    relays(0, 1, 4)
    for half in range(2):
        gather(1, half, 1)
    for s in range(2, 5):
        for kh in range(2):
            relays(1, kh, s)
    for ch in range(2):
        for half in range(2):
            for step, flip in first_order:
                first_hop(ch, half, step, flip).wait_send()
            for kh in range(2):
                for step in (1, 3, 2):
                    second_hop(ch, half, kh, step).wait_send()
                for side in range(2):
                    hop(ch, half, kh, side, hops_of(ch, side)).wait_recv()
                    for s in range(1, hops_of(ch, side) + 1):
                        hop(ch, half, kh, side, s).wait_send()


def cross_kernel(flag_ref, spec_ref, band_ref, partner_ref):
    own = pl.program_id(0)
    half = pl.program_id(1)
    for i in range(2):

        @pl.when(own == i)
        def _():
            def pair(g, _):
                row = pl.multiple_of(g * 8, 8)
                for kh in range(2):
                    cols = pl.ds(KX // 2 * kh, KX // 2)
                    re0 = spec_ref[4, i, half, kh, 0, pl.ds(row, 8), :]
                    im0 = spec_ref[4, i, half, kh, 1, pl.ds(row, 8), :]
                    for which, out, sign in ((0, band_ref, 1), (1, partner_ref, -1)):
                        for d in range(BAND):
                            off, odd = divmod(i + sign * d, 2)
                            re1 = spec_ref[4 + off, odd, half, kh, 0, pl.ds(row, 8), :]
                            im1 = spec_ref[4 + off, odd, half, kh, 1, pl.ds(row, 8), :]
                            at = (2 * which + i) * BAND + d
                            ask = jnp.broadcast_to(flag_ref[at : at + 1, :], (8, KX // 2)) != 0.0
                            re, im = re0 * re1 + im0 * im1, im0 * re1 - re0 * im1
                            out[0, d, 0, pl.ds(row, 8), cols] = jnp.where(ask, re, 0.0)
                            out[0, d, 1, pl.ds(row, 8), cols] = jnp.where(ask, im, 0.0)
                return 0

            lax.fori_loop(0, 2, pair, 0)


def local(velocity, plane_slot, pair_list):
    span, twist, axial_cat = [jnp.asarray(t) for t in tables()]
    vmem = pl.BlockSpec(memory_space=pltpu.VMEM)
    hbm = pl.BlockSpec(memory_space=pltpu.HBM)
    slab = (2, 2, 2, 2, 16, KX // 2)
    dma = pltpu.SemaphoreType.DMA
    spectra, flags = pl.pallas_call(
        transform_kernel,
        out_shape=(
            jax.ShapeDtypeStruct((9,) + slab, f32),
            jax.ShapeDtypeStruct((4 * BAND, KX // 2), f32),
        ),
        in_specs=[pl.BlockSpec(memory_space=pltpu.SMEM), hbm, hbm, hbm, hbm, vmem],
        out_specs=(vmem, vmem),
        scratch_shapes=[
            pltpu.VMEM((2, ROWS, NZ), f32),
            pltpu.VMEM((512, 256), bf16),
            pltpu.VMEM((CLASSES, 2, 256), f32),
            pltpu.VMEM((2, KX, DEPTH), bf16),
            pltpu.VMEM((2, 8, 16, 512), bf16),
            pltpu.VMEM((2, 8, 16, 512), bf16),
            pltpu.VMEM((2, 8, 16, 512), bf16),
            pltpu.VMEM((2, 8, 16, 512), bf16),
            pltpu.VMEM((2, 8, 16, 128), f32),
            pltpu.VMEM((2, 8, 16, 128), f32),
            pltpu.VMEM((2, CLASSES, ROWS, 128), f32),
            pltpu.VMEM((2, 2, 8, ROWS, 128), f32),
            pltpu.VMEM((2, 2, DEPTH, 256), bf16),
            pltpu.VMEM((2, KX, 256), f32),
            pltpu.VMEM((2, KX // 2, 128), f32),
            pltpu.VMEM((2, 2, 128, 128), f32),
            pltpu.VMEM((2, 2, 2, 4, 2, 16, KX // 2), f32),
            pltpu.VMEM((2, 2, 2, 4, 2, 16, KX // 2), f32),
            dma((2, ROWS // 32)),
            dma((3,)),
            dma((2, 2)),
            dma((2, 2, 8)),
            dma((2, 2, 8)),
            dma((2, 2, 2, 4)),
            dma((2, 2, 2, 4)),
            dma((2, 2, 2, 2, 5)),
            dma((2, 2, 2, 2, 5)),
        ],
        compiler_params=pltpu.CompilerParams(
            collective_id=0, has_side_effects=True, vmem_limit_bytes=40 * 1024 * 1024
        ),
        name="transform",
    )(*[
        pltpu.with_memory_space_constraint(array, pltpu.HBM)
        for array in (plane_slot, velocity, span, twist, axial_cat, pair_list.T)
    ])

    share = KZ // PEERS
    out = jax.ShapeDtypeStruct((2, BAND, 2, share, KX), f32)
    block = pl.BlockSpec((1, BAND, 2, share // 2, KX), lambda i, h: (i, 0, 0, h, 0))
    band_cross, partner_cross = pl.pallas_call(
        cross_kernel,
        grid=(2, 2),
        out_shape=(out, out),
        in_specs=[vmem, vmem],
        out_specs=(block, block),
        compiler_params=pltpu.CompilerParams(vmem_limit_bytes=24 * 1024 * 1024),
        name="cross",
    )(flags, spectra)
    return (band_cross, partner_cross)


def solution(mesh):
    return jax.shard_map(
        local,
        mesh=mesh,
        in_specs=(P("plane", "pencil", None), P(), P()),
        out_specs=(P("plane", None, None, "pencil", None), P("plane", None, None, "pencil", None)),
        check_vma=False,
    )
```

```python
import functools
import math

import jax
import jax.numpy as jnp
import numpy as np
from jax import lax
from jax.experimental import pallas as pl
from jax.experimental.pallas import tpu as pltpu
from jax.sharding import PartitionSpec as P

NX = 5120
NZ = 3840
KX = 512
KZ = 1024
BAND = 8
CLASSES = 16
SPAN = NZ // CLASSES
PEERS = 32
RINGS = 8
ROWS = NX // PEERS
DEPTH = 1024
MESH = pl.DeviceIdType.MESH
bf16 = jnp.bfloat16
f32 = jnp.float32


def split_np(table):
    high = np.asarray(table, np.float32).astype(bf16)
    low = (table - high.astype(np.float64)).astype(np.float32).astype(bf16)
    return high, low


@functools.cache
def tables():
    lane = np.arange(128)
    route, other, ri = lane // 8, lane // 2 % 4, lane % 2
    first, group, core = route // 8, route // 2 % 4, route % 2
    x_at = np.where(first == 0, other, group)
    y_at = np.where(first == 0, group, other)
    m = 2 * (x_at * 8 + y_at * 2 + core) + first
    z = np.arange(256)
    phase = 2 * np.pi * ((z[:, None] * m[None, :]) % SPAN) / SPAN
    real_rows = np.where(ri == 0, np.cos(phase), -np.sin(phase))
    imag_rows = np.where(ri == 0, np.sin(phase), np.cos(phase))
    inside = (z < SPAN)[:, None]
    span = np.concatenate([real_rows * inside, imag_rows * inside], axis=0)

    c = np.arange(CLASSES)
    turn = 2 * np.pi * (c[:, None] * z[None, :]) / NZ
    keep = (z < SPAN)[None, :]
    twist = np.stack([np.cos(turn) * keep, np.sin(turn) * keep], axis=1).astype(np.float32)

    k = np.arange(KX)
    kx = np.where(k < KX // 2, k, k - KX)
    r = np.arange(2 * ROWS)
    theta = 2 * np.pi * ((kx[:, None] * r[None, :]) % NX) / NX
    ax_hi, ax_lo = split_np(np.concatenate([np.cos(theta), np.sin(theta)], axis=0))
    parts = []
    for core in range(2):
        rows = slice(core * ROWS, core * ROWS + ROWS)
        parts += [ax_hi[:, rows], ax_hi[:, rows], ax_lo[:, rows]]
    parts.append(np.zeros((2 * KX, DEPTH - 6 * ROWS), bf16))
    axial = np.concatenate(parts, axis=1).reshape(2, 2, KX // 2, DEPTH)
    axial = np.ascontiguousarray(axial.transpose(1, 0, 2, 3)).reshape(2, KX, DEPTH)
    return np.concatenate(split_np(span), axis=1), twist, axial


def times(a, w):
    ar, ai = a
    wr, wi = w
    s = math.sqrt(0.5)
    if abs(wr - 1) < 1e-12:
        return a
    if abs(wr) < 1e-12 and abs(wi + 1) < 1e-12:
        return (ai, None if ar is None else -ar)
    if abs(wr - s) < 1e-12 and abs(wi + s) < 1e-12 and ai is not None:
        return ((ar + ai) * s, (ai - ar) * s)
    if ai is None:
        return (ar * wr, ar * wi)
    return (ar * wr - ai * wi, ar * wi + ai * wr)


def add(a, b):
    if a is None:
        return b
    if b is None:
        return a
    return a + b


def sub(a, b):
    if b is None:
        return a
    if a is None:
        return -b
    return a - b


def real_fft(xs):
    n = len(xs)
    if n == 1:
        return [(xs[0], None)]
    even = real_fft(xs[0::2])
    odd = real_fft(xs[1::2])
    out = [None] * (n // 2 + 1)
    for k in range(n // 4 + 1):
        w = (math.cos(2 * math.pi * k / n), -math.sin(2 * math.pi * k / n))
        er, ei = even[k]
        tr, ti = times(odd[k], w)
        out[k] = (add(er, tr), add(ei, ti))
        if n // 2 - k != k:
            out[n // 2 - k] = (sub(er, tr), sub(ti, ei))
    return out


def twisted_pair(modes, i, cos_of, sin_of):
    stack = lambda u, v: jnp.concatenate([u, v], axis=0)
    a, b = modes[i]
    if i == 0:
        e = modes[8][0]
        return stack(a, e * cos_of(8)), stack(jnp.zeros_like(a), -(e * sin_of(8)))
    tc, ts = cos_of(i), sin_of(i)
    uc, us = cos_of(16 - i), sin_of(16 - i)
    return stack(a * tc + b * ts, a * uc - b * us), stack(b * tc - a * ts, -(b * uc + a * us))


def split(x):
    high = x.astype(bf16)
    return high, (x - high.astype(f32)).astype(bf16)


def lane_exchange(tiles, lane, roll):
    turned = [t if c == 0 else roll(t, 8 * c) for c, t in enumerate(tiles)]
    tiles = [turned[-j % 16] for j in range(16)]
    for bit in range(4):
        gap = 1 << bit
        high_block = (lane & (8 * gap)) != 0
        tiles = [jnp.where(high_block, tiles[j - gap], tiles[j]) for j in range(16)]
    return tiles


def lane_roll(x, shift):
    return pltpu.roll(x, shift, 1)


def transform_kernel(
    slot_ref, vel_hbm, span_hbm, twist_hbm, axial_hbm, pair_ref, out_ref, flag_ref,
    vel, span_ref, twist_ref, axial_ref, hi_even, lo_even, hi_odd, lo_odd, z_even, z_odd, send_buf, recv_buf, v_cat, q_buf, turn_buf,
    flip_buf, part_buf, sum_buf, load_sem, table_sem, own_sem, a_send, a_recv, b_send, b_recv,
    z_send, z_recv,
):
    me = lax.axis_index("pencil")
    ring = lax.axis_index("plane")
    below = lax.rem(ring + RINGS - 1, RINGS)
    above = lax.rem(ring + 1, RINGS)
    core = lax.rem(me, 2)
    y_at = lax.rem(me // 2, 4)
    x_at = me // 8
    place = (y_at, x_at)
    across = (x_at, y_at)

    def member(half, group, core_at):
        if half == 0:
            return x_at * 8 + group * 2 + core_at
        return group * 8 + y_at * 2 + core_at

    barrier = pltpu.get_barrier_semaphore()

    def load(slot, part):
        rows = pl.ds(part * 32, 32)
        return pltpu.make_async_copy(
            vel_hbm.at[slot, rows], vel.at[slot, rows], load_sem.at[slot, part]
        )

    twist_in = pltpu.make_async_copy(twist_hbm, twist_ref, table_sem.at[0])
    span_in = pltpu.make_async_copy(span_hbm, span_ref, table_sem.at[1])
    tables_in = pltpu.make_async_copy(axial_hbm, axial_ref, table_sem.at[2])
    twist_in.start()
    for part in range(ROWS // 32):
        for slot in range(2):
            load(slot, part).start()
        if part == 0:
            span_in.start()
    tables_in.start()
    for half in range(2):
        for step in range(4):
            for flip in range(2):
                if step == 0 and (flip == 0 or half == 1):
                    continue
                peer = member(half, lax.rem(place[half] + step, 4), lax.rem(core + flip, 2))
                pl.semaphore_signal(barrier, inc=1, device_id=(ring, peer), device_id_type=MESH)
    for other in (below, above):
        pl.semaphore_signal(barrier, inc=1, device_id=(other, me), device_id_type=MESH)
    for half in range(2):
        for s in range(2):
            rest = pl.ds(6 * ROWS, DEPTH - 6 * ROWS)
            v_cat[half, s, rest, :] = jnp.zeros((DEPTH - 6 * ROWS, 256), bf16)

    lane8 = lax.broadcasted_iota(jnp.int32, (8, 128), 1)
    groups = ROWS // 16

    def residues(g, y_hi, y_lo):
        slot = lax.rem(slot_ref[2 * ring + g // groups], 2)
        row = pl.multiple_of(lax.rem(g, groups) * 16, 16)

        def tile(k, half):
            at = (pl.ds(row + 8 * half, 8), pl.ds(128 * (k % 30), 128))
            return jnp.where(slot == 0, vel[(0,) + at], vel[(1,) + at])

        for part, half in ((0, 0), (0, 1), (1, 0), (1, 1)):
            xs = []
            for j in range(CLASSES):
                first, shift = divmod(SPAN * j + 128 * part, 128)
                if shift == 0:
                    xs.append(tile(first, half))
                    continue
                xs.append(
                    jnp.where(
                        lane8 < 128 - shift,
                        lane_roll(tile(first, half), 128 - shift),
                        lane_roll(tile(first + 1, half), 128 - shift),
                    )
                )
            cols = pl.ds(128 * part, 128)
            cos_of = lambda c: jnp.broadcast_to(twist_ref[c, 0:1, cols], (8, 128))
            sin_of = lambda c: jnp.broadcast_to(twist_ref[c, 1:2, cols], (8, 128))
            modes = real_fft(xs)
            for i in range(8):
                for which, value in enumerate(twisted_pair(modes, i, cos_of, sin_of)):
                    at = pl.ds(256 * which + 128 * part, 128)
                    y_hi[half, i, :, at], y_lo[half, i, :, at] = split(value)

    def products(y_hi, y_lo, z_buf):
        high = y_hi[...].reshape(CLASSES * 16, 512)
        low = y_lo[...].reshape(CLASSES * 16, 512)
        both = jnp.dot(high, span_ref[...], preferred_element_type=f32)
        total = both[:, :128] + both[:, 128:]
        total += jnp.dot(low, span_ref[:, pl.ds(0, 128)], preferred_element_type=f32)
        z_buf[...] = total.reshape(2, 8, 16, 128)

    def regroup(g, z_buf):
        g = jnp.maximum(g, 0)
        row = pl.multiple_of(lax.rem(g, groups) * 16, 16)
        for part in range(2):
            tiles = [z_buf[part, min(c, 16 - c) % 8, pl.ds(c // 8 * 8, 8), :] for c in range(CLASSES)]
            for f, tile in enumerate(lane_exchange(tiles, lane8, lane_roll)):
                send_buf[g // groups, f, pl.ds(row + 8 * part, 8), :] = tile

    def own_copy(ch, half):
        mine = place[half] * 2 + core
        return pltpu.make_async_copy(
            send_buf.at[ch, 8 * half + mine], recv_buf.at[ch, half, mine], own_sem.at[ch, half]
        )

    def first_hop(ch, half, step, flip, back=False, rows=pl.ds(0, ROWS)):
        mine = place[half] * 2 + core
        group = lax.rem(place[half] + step, 4)
        core_at = lax.rem(core + flip, 2)
        peer = group * 2 + core_at
        return pltpu.make_async_remote_copy(
            src_ref=send_buf.at[ch, 8 * half + peer, rows],
            dst_ref=recv_buf.at[ch, half, peer if back else mine, rows],
            send_sem=a_send.at[ch, half, 2 * step + flip],
            recv_sem=a_recv.at[ch, half, peer if back else mine],
            device_id=(ring, member(half, group, core_at)),
            device_id_type=MESH,
        )

    def second_hop(ch, half, kh, step, back=False):
        there = lax.rem(across[half] + step, 4)
        return pltpu.make_async_remote_copy(
            src_ref=part_buf.at[ch, half, kh, there],
            dst_ref=sum_buf.at[ch, half, kh, there if back else across[half]],
            send_sem=b_send.at[ch, half, kh, step],
            recv_sem=b_recv.at[ch, half, kh, there if back else across[half]],
            device_id=(ring, member(1 - half, there, core)),
            device_id_type=MESH,
        )

    first_order = ((1, 0), (3, 0), (1, 1), (3, 1), (2, 0), (2, 1), (0, 1))

    parts = (pl.ds(0, 32), pl.ds(32, 64), pl.ds(96, 64))

    def send_part(ch, part):
        if part == 2:
            for half in range(2):
                own_copy(ch, half).start()
        for step, flip in first_order:
            for half in range(2):
                first_hop(ch, half, step, flip, rows=parts[part]).start()

    def hop(ch, half, kh, side, s):
        sign = 1 if side == 0 else -1
        return pltpu.make_async_remote_copy(
            src_ref=out_ref.at[4 + sign * (s - 1), ch, half, kh],
            dst_ref=out_ref.at[4 + sign * s, ch, half, kh],
            send_sem=z_send.at[ch, half, kh, side, s],
            recv_sem=z_recv.at[ch, half, kh, side, s],
            device_id=(below if side == 0 else above, me),
            device_id_type=MESH,
        )

    def hops_of(ch, side):
        return 4 if ch == side else 3

    def relay(ch, half, kh, s):
        for side in range(2):
            if s > hops_of(ch, side):
                continue
            if s > 1:
                hop(ch, half, kh, side, s - 1).wait_recv()
            hop(ch, half, kh, side, s).start()

    def relays(ch, kh, s):
        for half in range(2):
            relay(ch, half, kh, s)

    def collect(ch, half):
        own_copy(ch, half).wait()
        for step, flip in first_order:
            first_hop(ch, half, step, flip, back=True).wait_recv()
        for s in range(2):
            for o in range(2):
                cols = pl.ds(128 * o, 128)
                for c in range(2):
                    high, low = split(recv_buf[ch, half, 4 * s + 2 * o + c])
                    v_cat[half, s, pl.ds(3 * c * ROWS, ROWS), cols] = high
                    v_cat[half, s, pl.ds((3 * c + 1) * ROWS, ROWS), cols] = low
                    v_cat[half, s, pl.ds((3 * c + 2) * ROWS, ROWS), cols] = high

    def axial(ch, half, kh):
        for s in range(2):
            q_buf[s] = jnp.dot(axial_ref[kh], v_cat[half, s], preferred_element_type=f32)

        k = lax.broadcasted_iota(jnp.int32, (16, 256), 0)
        o = lax.broadcasted_iota(jnp.int32, (16, 256), 1) // 128
        scale = 1.0 / math.sqrt(NX * NZ)
        cos_of, sin_of = [], []
        for s in range(2):
            group = 2 * s + o
            steps = 4 * x_at + group if half == 0 else 4 * group + y_at
            psi = lax.rem(k * steps, 16).astype(f32) * (2.0 * math.pi / 16)
            cos_of.append(jnp.cos(psi) * scale)
            sin_of.append(jnp.sin(psi) * scale)
        lane = lax.broadcasted_iota(jnp.int32, (16, 128), 1)
        even = lane % 2 == 0
        mine = 8 * half + place[half] * 2 + core
        shift = lax.rem(128 - 8 * mine, 128)
        for blk in range(KX // 32):
            p = q = 0.0
            for s in range(2):
                a = q_buf[s, pl.ds(16 * blk, 16), :]
                b = q_buf[s, pl.ds(KX // 2 + 16 * blk, 16), :]
                p = p + (a * cos_of[s] - b * sin_of[s])
                q = q + (a * sin_of[s] + b * cos_of[s])
            p = p[:, :128] + p[:, 128:]
            q = q[:, :128] + q[:, 128:]
            q = jnp.where(even, -q, q)
            turn_buf[0, pl.ds(16 * blk, 16), :] = lane_roll(p, shift)
            turn_buf[1, pl.ds(16 * blk, 16), :] = lane_roll(q, shift)
        for blk in range(2):
            rows = pl.ds(128 * blk, 128)
            for which in range(2):
                flip_buf[which, blk] = turn_buf[which, rows, :].T
            for there in range(4):
                for ri in range(2):
                    straight = flip_buf[0, blk, pl.ds(2 * there + ri, 16, stride=8), :]
                    crossed = flip_buf[1, blk, pl.ds(2 * there + 1 - ri, 16, stride=8), :]
                    part_buf[ch, half, kh, there, ri, :, rows] = straight + crossed
        for step in (1, 3, 2):
            second_hop(ch, half, kh, step).start()

    def gather(ch, half, kh):
        total = part_buf[ch, half, kh, across[half]]
        for step in (1, 3, 2):
            second_hop(ch, half, kh, step, back=True).wait_recv()
        for step in range(1, 4):
            total = total + sum_buf[ch, half, kh, lax.rem(across[half] + step, 4)]
        out_ref[4, ch, half, kh] = total
        relay(ch, half, kh, 1)

    def body(q, _):
        @pl.when(q < groups // 2)
        def _():
            for s in range(2):
                load(s, q).wait()

        for odd in range(2):
            regroup(2 * q + odd - 2, (z_even, z_odd)[odd])
            if odd == 0:
                products(hi_odd, lo_odd, z_odd)
                residues(2 * q, hi_even, lo_even)
            else:
                products(hi_even, lo_even, z_even)
                residues(2 * q + 1, hi_odd, lo_odd)

        @pl.when(q == 1)
        def _():
            pl.semaphore_wait(barrier, 15)
            send_part(0, 0)

        for at, ch, part in ((3, 0, 1), (5, 0, 2), (6, 1, 0), (8, 1, 1)):

            @pl.when(q == at)
            def _():
                send_part(ch, part)

        return 0

    twist_in.wait()
    span_in.wait()
    lax.fori_loop(0, groups, body, 0)
    regroup(2 * groups - 2, z_even)
    products(hi_odd, lo_odd, z_odd)
    regroup(2 * groups - 1, z_odd)
    index = lax.broadcasted_iota(jnp.int32, (4 * BAND, 1), 0)
    own_plane = 2 * ring + index // BAND % 2
    gap = index % BAND
    code = jnp.where(index < 2 * BAND, own_plane, own_plane - gap) * BAND + gap
    lower = pair_ref[0:1, :]
    asked = lower * BAND + pair_ref[1:2, :] - lower == code
    asked = jnp.max(jnp.where(asked, 1.0, 0.0), axis=1, keepdims=True)
    asked = jnp.where((index >= 2 * BAND) & (own_plane < gap), 0.0, asked)
    flag_ref[...] = jnp.broadcast_to(asked, (4 * BAND, KX // 2))
    tables_in.wait()
    collect(0, 0)
    axial(0, 0, 0)
    collect(0, 1)
    axial(0, 1, 0)
    axial(0, 0, 1)
    axial(0, 1, 1)
    send_part(1, 2)
    for kh in range(2):
        for half in range(2):
            gather(0, half, kh)
    for kh in range(2):
        relays(0, kh, 2)
    collect(1, 0)
    axial(1, 0, 0)
    relays(0, 0, 3)
    collect(1, 1)
    axial(1, 1, 0)
    relays(0, 1, 3)
    axial(1, 0, 1)
    axial(1, 1, 1)
    relays(0, 0, 4)
    for half in range(2):
        gather(1, half, 0)
    relays(0, 1, 4)
    for half in range(2):
        gather(1, half, 1)
    for s in range(2, 5):
        for kh in range(2):
            relays(1, kh, s)
    for ch in range(2):
        for half in range(2):
            for step, flip in first_order:
                first_hop(ch, half, step, flip).wait_send()
            for kh in range(2):
                for step in (1, 3, 2):
                    second_hop(ch, half, kh, step).wait_send()
                for side in range(2):
                    hop(ch, half, kh, side, hops_of(ch, side)).wait_recv()
                    for s in range(1, hops_of(ch, side) + 1):
                        hop(ch, half, kh, side, s).wait_send()


def cross_kernel(flag_ref, spec_ref, band_ref, partner_ref):
    own = pl.program_id(0)
    half = pl.program_id(1)
    for i in range(2):

        @pl.when(own == i)
        def _():
            def pair(g, _):
                row = pl.multiple_of(g * 8, 8)
                for kh in range(2):
                    cols = pl.ds(KX // 2 * kh, KX // 2)
                    re0 = spec_ref[4, i, half, kh, 0, pl.ds(row, 8), :]
                    im0 = spec_ref[4, i, half, kh, 1, pl.ds(row, 8), :]
                    for which, out, sign in ((0, band_ref, 1), (1, partner_ref, -1)):
                        for d in range(BAND):
                            off, odd = divmod(i + sign * d, 2)
                            re1 = spec_ref[4 + off, odd, half, kh, 0, pl.ds(row, 8), :]
                            im1 = spec_ref[4 + off, odd, half, kh, 1, pl.ds(row, 8), :]
                            at = (2 * which + i) * BAND + d
                            ask = jnp.broadcast_to(flag_ref[at : at + 1, :], (8, KX // 2)) != 0.0
                            re, im = re0 * re1 + im0 * im1, im0 * re1 - re0 * im1
                            out[0, d, 0, pl.ds(row, 8), cols] = jnp.where(ask, re, 0.0)
                            out[0, d, 1, pl.ds(row, 8), cols] = jnp.where(ask, im, 0.0)
                return 0

            lax.fori_loop(0, 2, pair, 0)


def local(velocity, plane_slot, pair_list):
    span, twist, axial_cat = [jnp.asarray(t) for t in tables()]
    vmem = pl.BlockSpec(memory_space=pltpu.VMEM)
    hbm = pl.BlockSpec(memory_space=pltpu.HBM)
    slab = (2, 2, 2, 2, 16, KX // 2)
    dma = pltpu.SemaphoreType.DMA
    spectra, flags = pl.pallas_call(
        transform_kernel,
        out_shape=(
            jax.ShapeDtypeStruct((9,) + slab, f32),
            jax.ShapeDtypeStruct((4 * BAND, KX // 2), f32),
        ),
        in_specs=[pl.BlockSpec(memory_space=pltpu.SMEM), hbm, hbm, hbm, hbm, vmem],
        out_specs=(vmem, vmem),
        scratch_shapes=[
            pltpu.VMEM((2, ROWS, NZ), f32),
            pltpu.VMEM((512, 256), bf16),
            pltpu.VMEM((CLASSES, 2, 256), f32),
            pltpu.VMEM((2, KX, DEPTH), bf16),
            pltpu.VMEM((2, 8, 16, 512), bf16),
            pltpu.VMEM((2, 8, 16, 512), bf16),
            pltpu.VMEM((2, 8, 16, 512), bf16),
            pltpu.VMEM((2, 8, 16, 512), bf16),
            pltpu.VMEM((2, 8, 16, 128), f32),
            pltpu.VMEM((2, 8, 16, 128), f32),
            pltpu.VMEM((2, CLASSES, ROWS, 128), f32),
            pltpu.VMEM((2, 2, 8, ROWS, 128), f32),
            pltpu.VMEM((2, 2, DEPTH, 256), bf16),
            pltpu.VMEM((2, KX, 256), f32),
            pltpu.VMEM((2, KX // 2, 128), f32),
            pltpu.VMEM((2, 2, 128, 128), f32),
            pltpu.VMEM((2, 2, 2, 4, 2, 16, KX // 2), f32),
            pltpu.VMEM((2, 2, 2, 4, 2, 16, KX // 2), f32),
            dma((2, ROWS // 32)),
            dma((3,)),
            dma((2, 2)),
            dma((2, 2, 8)),
            dma((2, 2, 8)),
            dma((2, 2, 2, 4)),
            dma((2, 2, 2, 4)),
            dma((2, 2, 2, 2, 5)),
            dma((2, 2, 2, 2, 5)),
        ],
        compiler_params=pltpu.CompilerParams(
            collective_id=0, has_side_effects=True, vmem_limit_bytes=40 * 1024 * 1024
        ),
        name="transform",
    )(*[
        pltpu.with_memory_space_constraint(array, pltpu.HBM)
        for array in (plane_slot, velocity, span, twist, axial_cat, pair_list.T)
    ])

    share = KZ // PEERS
    out = jax.ShapeDtypeStruct((2, BAND, 2, share, KX), f32)
    block = pl.BlockSpec((1, BAND, 2, share // 2, KX), lambda i, h: (i, 0, 0, h, 0))
    band_cross, partner_cross = pl.pallas_call(
        cross_kernel,
        grid=(2, 2),
        out_shape=(out, out),
        in_specs=[vmem, vmem],
        out_specs=(block, block),
        compiler_params=pltpu.CompilerParams(vmem_limit_bytes=24 * 1024 * 1024),
        name="cross",
    )(flags, spectra)
    return (band_cross, partner_cross)


def solution(mesh):
    return jax.shard_map(
        local,
        mesh=mesh,
        in_specs=(P("plane", "pencil", None), P(), P()),
        out_specs=(P("plane", None, None, "pencil", None), P("plane", None, None, "pencil", None)),
        check_vma=False,
    )
```

```python
import functools
import math

import jax
import jax.numpy as jnp
import numpy as np
from jax import lax
from jax.experimental import pallas as pl
from jax.experimental.pallas import tpu as pltpu
from jax.sharding import PartitionSpec as P

NX = 5120
NZ = 3840
KX = 512
KZ = 1024
BAND = 8
CLASSES = 16
SPAN = NZ // CLASSES
PEERS = 32
RINGS = 8
ROWS = NX // PEERS
DEPTH = 1024
MESH = pl.DeviceIdType.MESH
bf16 = jnp.bfloat16
f32 = jnp.float32


def split_np(table):
    high = np.asarray(table, np.float32).astype(bf16)
    low = (table - high.astype(np.float64)).astype(np.float32).astype(bf16)
    return high, low


@functools.cache
def tables():
    lane = np.arange(128)
    route, other, ri = lane // 8, lane // 2 % 4, lane % 2
    first, group, core = route // 8, route // 2 % 4, route % 2
    x_at = np.where(first == 0, other, group)
    y_at = np.where(first == 0, group, other)
    m = 2 * (x_at * 8 + y_at * 2 + core) + first
    z = np.arange(256)
    phase = 2 * np.pi * ((z[:, None] * m[None, :]) % SPAN) / SPAN
    real_rows = np.where(ri == 0, np.cos(phase), -np.sin(phase))
    imag_rows = np.where(ri == 0, np.sin(phase), np.cos(phase))
    inside = (z < SPAN)[:, None]
    span = np.concatenate([real_rows * inside, imag_rows * inside], axis=0)

    c = np.arange(CLASSES)
    turn = 2 * np.pi * (c[:, None] * z[None, :]) / NZ
    keep = (z < SPAN)[None, :]
    twist = np.stack([np.cos(turn) * keep, np.sin(turn) * keep], axis=1).astype(np.float32)

    k = np.arange(KX)
    kx = np.where(k < KX // 2, k, k - KX)
    r = np.arange(2 * ROWS)
    theta = 2 * np.pi * ((kx[:, None] * r[None, :]) % NX) / NX
    ax_hi, ax_lo = split_np(np.concatenate([np.cos(theta), np.sin(theta)], axis=0))
    parts = []
    for core in range(2):
        rows = slice(core * ROWS, core * ROWS + ROWS)
        parts += [ax_hi[:, rows], ax_hi[:, rows], ax_lo[:, rows]]
    parts.append(np.zeros((2 * KX, DEPTH - 6 * ROWS), bf16))
    axial = np.concatenate(parts, axis=1).reshape(2, 2, KX // 2, DEPTH)
    axial = np.ascontiguousarray(axial.transpose(1, 0, 2, 3)).reshape(2, KX, DEPTH)
    return np.concatenate(split_np(span), axis=1), twist, axial


def times(a, w):
    ar, ai = a
    wr, wi = w
    s = math.sqrt(0.5)
    if abs(wr - 1) < 1e-12:
        return a
    if abs(wr) < 1e-12 and abs(wi + 1) < 1e-12:
        return (ai, None if ar is None else -ar)
    if abs(wr - s) < 1e-12 and abs(wi + s) < 1e-12 and ai is not None:
        return ((ar + ai) * s, (ai - ar) * s)
    if ai is None:
        return (ar * wr, ar * wi)
    return (ar * wr - ai * wi, ar * wi + ai * wr)


def add(a, b):
    if a is None:
        return b
    if b is None:
        return a
    return a + b


def sub(a, b):
    if b is None:
        return a
    if a is None:
        return -b
    return a - b


def real_fft(xs):
    n = len(xs)
    if n == 1:
        return [(xs[0], None)]
    even = real_fft(xs[0::2])
    odd = real_fft(xs[1::2])
    out = [None] * (n // 2 + 1)
    for k in range(n // 4 + 1):
        w = (math.cos(2 * math.pi * k / n), -math.sin(2 * math.pi * k / n))
        er, ei = even[k]
        tr, ti = times(odd[k], w)
        out[k] = (add(er, tr), add(ei, ti))
        if n // 2 - k != k:
            out[n // 2 - k] = (sub(er, tr), sub(ti, ei))
    return out


def twisted_pair(modes, i, cos_of, sin_of):
    stack = lambda u, v: jnp.concatenate([u, v], axis=0)
    a, b = modes[i]
    if i == 0:
        e = modes[8][0]
        return stack(a, e * cos_of(8)), stack(jnp.zeros_like(a), -(e * sin_of(8)))
    tc, ts = cos_of(i), sin_of(i)
    uc, us = cos_of(16 - i), sin_of(16 - i)
    return stack(a * tc + b * ts, a * uc - b * us), stack(b * tc - a * ts, -(b * uc + a * us))


def split(x):
    high = x.astype(bf16)
    return high, (x - high.astype(f32)).astype(bf16)


def lane_exchange(tiles, lane, roll):
    turned = [t if c == 0 else roll(t, 8 * c) for c, t in enumerate(tiles)]
    tiles = [turned[-j % 16] for j in range(16)]
    for bit in range(4):
        gap = 1 << bit
        high_block = (lane & (8 * gap)) != 0
        tiles = [jnp.where(high_block, tiles[j - gap], tiles[j]) for j in range(16)]
    return tiles


def lane_roll(x, shift):
    return pltpu.roll(x, shift, 1)


def transform_kernel(
    slot_ref, vel_hbm, span_hbm, twist_hbm, axial_hbm, pair_ref, out_ref, flag_ref,
    vel, span_ref, twist_ref, axial_ref, hi_even, lo_even, hi_odd, lo_odd, z_even, z_odd, send_buf, recv_buf, v_cat, q_buf, turn_buf,
    flip_buf, part_buf, sum_buf, load_sem, table_sem, own_sem, a_send, a_recv, b_send, b_recv,
    z_send, z_recv,
):
    me = lax.axis_index("pencil")
    ring = lax.axis_index("plane")
    below = lax.rem(ring + RINGS - 1, RINGS)
    above = lax.rem(ring + 1, RINGS)
    core = lax.rem(me, 2)
    y_at = lax.rem(me // 2, 4)
    x_at = me // 8
    place = (y_at, x_at)
    across = (x_at, y_at)

    def member(half, group, core_at):
        if half == 0:
            return x_at * 8 + group * 2 + core_at
        return group * 8 + y_at * 2 + core_at

    barrier = pltpu.get_barrier_semaphore()

    def load(slot, part):
        rows = pl.ds(part * 32, 32)
        return pltpu.make_async_copy(
            vel_hbm.at[slot, rows], vel.at[slot, rows], load_sem.at[slot, part]
        )

    twist_in = pltpu.make_async_copy(twist_hbm, twist_ref, table_sem.at[0])
    span_in = pltpu.make_async_copy(span_hbm, span_ref, table_sem.at[1])
    tables_in = pltpu.make_async_copy(axial_hbm, axial_ref, table_sem.at[2])
    twist_in.start()
    for part in range(ROWS // 32):
        for slot in range(2):
            load(slot, part).start()
        if part == 0:
            span_in.start()
    tables_in.start()
    for half in range(2):
        for step in range(4):
            for flip in range(2):
                if step == 0 and (flip == 0 or half == 1):
                    continue
                peer = member(half, lax.rem(place[half] + step, 4), lax.rem(core + flip, 2))
                pl.semaphore_signal(barrier, inc=1, device_id=(ring, peer), device_id_type=MESH)
    for other in (below, above):
        pl.semaphore_signal(barrier, inc=1, device_id=(other, me), device_id_type=MESH)
    for half in range(2):
        for s in range(2):
            rest = pl.ds(6 * ROWS, DEPTH - 6 * ROWS)
            v_cat[half, s, rest, :] = jnp.zeros((DEPTH - 6 * ROWS, 256), bf16)

    lane8 = lax.broadcasted_iota(jnp.int32, (8, 128), 1)
    groups = ROWS // 16

    def residues(g, y_hi, y_lo):
        slot = lax.rem(slot_ref[2 * ring + g // groups], 2)
        row = pl.multiple_of(lax.rem(g, groups) * 16, 16)

        def tile(k, half):
            at = (pl.ds(row + 8 * half, 8), pl.ds(128 * (k % 30), 128))
            return jnp.where(slot == 0, vel[(0,) + at], vel[(1,) + at])

        for part, half in ((0, 0), (0, 1), (1, 0), (1, 1)):
            xs = []
            for j in range(CLASSES):
                first, shift = divmod(SPAN * j + 128 * part, 128)
                if shift == 0:
                    xs.append(tile(first, half))
                    continue
                xs.append(
                    jnp.where(
                        lane8 < 128 - shift,
                        lane_roll(tile(first, half), 128 - shift),
                        lane_roll(tile(first + 1, half), 128 - shift),
                    )
                )
            cols = pl.ds(128 * part, 128)
            cos_of = lambda c: jnp.broadcast_to(twist_ref[c, 0:1, cols], (8, 128))
            sin_of = lambda c: jnp.broadcast_to(twist_ref[c, 1:2, cols], (8, 128))
            modes = real_fft(xs)
            for i in range(8):
                for which, value in enumerate(twisted_pair(modes, i, cos_of, sin_of)):
                    at = pl.ds(256 * which + 128 * part, 128)
                    y_hi[half, i, :, at], y_lo[half, i, :, at] = split(value)

    def products(y_hi, y_lo, z_buf):
        high = y_hi[...].reshape(CLASSES * 16, 512)
        low = y_lo[...].reshape(CLASSES * 16, 512)
        both = jnp.dot(high, span_ref[...], preferred_element_type=f32)
        total = both[:, :128] + both[:, 128:]
        total += jnp.dot(low, span_ref[:, pl.ds(0, 128)], preferred_element_type=f32)
        z_buf[...] = total.reshape(2, 8, 16, 128)

    def regroup(g, z_buf):
        g = jnp.maximum(g, 0)
        row = pl.multiple_of(lax.rem(g, groups) * 16, 16)
        for part in range(2):
            tiles = [z_buf[part, min(c, 16 - c) % 8, pl.ds(c // 8 * 8, 8), :] for c in range(CLASSES)]
            for f, tile in enumerate(lane_exchange(tiles, lane8, lane_roll)):
                send_buf[g // groups, f, pl.ds(row + 8 * part, 8), :] = tile

    def own_copy(ch, half):
        mine = place[half] * 2 + core
        return pltpu.make_async_copy(
            send_buf.at[ch, 8 * half + mine], recv_buf.at[ch, half, mine], own_sem.at[ch, half]
        )

    def first_hop(ch, half, step, flip, back=False, rows=pl.ds(0, ROWS)):
        mine = place[half] * 2 + core
        group = lax.rem(place[half] + step, 4)
        core_at = lax.rem(core + flip, 2)
        peer = group * 2 + core_at
        return pltpu.make_async_remote_copy(
            src_ref=send_buf.at[ch, 8 * half + peer, rows],
            dst_ref=recv_buf.at[ch, half, peer if back else mine, rows],
            send_sem=a_send.at[ch, half, 2 * step + flip],
            recv_sem=a_recv.at[ch, half, peer if back else mine],
            device_id=(ring, member(half, group, core_at)),
            device_id_type=MESH,
        )

    def second_hop(ch, half, kh, step, back=False):
        there = lax.rem(across[half] + step, 4)
        return pltpu.make_async_remote_copy(
            src_ref=part_buf.at[ch, half, kh, there],
            dst_ref=sum_buf.at[ch, half, kh, there if back else across[half]],
            send_sem=b_send.at[ch, half, kh, step],
            recv_sem=b_recv.at[ch, half, kh, there if back else across[half]],
            device_id=(ring, member(1 - half, there, core)),
            device_id_type=MESH,
        )

    first_order = ((1, 0), (3, 0), (1, 1), (3, 1), (2, 0), (2, 1), (0, 1))

    parts = (pl.ds(0, 32), pl.ds(32, 64), pl.ds(96, 64))

    def send_part(ch, part):
        if part == 2:
            for half in range(2):
                own_copy(ch, half).start()
        for step, flip in first_order:
            for half in range(2):
                first_hop(ch, half, step, flip, rows=parts[part]).start()

    def hop(ch, half, kh, side, s):
        sign = 1 if side == 0 else -1
        return pltpu.make_async_remote_copy(
            src_ref=out_ref.at[4 + sign * (s - 1), ch, half, kh],
            dst_ref=out_ref.at[4 + sign * s, ch, half, kh],
            send_sem=z_send.at[ch, half, kh, side, s],
            recv_sem=z_recv.at[ch, half, kh, side, s],
            device_id=(below if side == 0 else above, me),
            device_id_type=MESH,
        )

    def hops_of(ch, side):
        return 4 if ch == side else 3

    def relay(ch, half, kh, s):
        for side in range(2):
            if s > hops_of(ch, side):
                continue
            if s > 1:
                hop(ch, half, kh, side, s - 1).wait_recv()
            hop(ch, half, kh, side, s).start()

    def relays(ch, kh, s):
        for half in range(2):
            relay(ch, half, kh, s)

    def collect(ch, half):
        own_copy(ch, half).wait()
        for step, flip in first_order:
            first_hop(ch, half, step, flip, back=True).wait_recv()
        for s in range(2):
            for o in range(2):
                cols = pl.ds(128 * o, 128)
                for c in range(2):
                    high, low = split(recv_buf[ch, half, 4 * s + 2 * o + c])
                    v_cat[half, s, pl.ds(3 * c * ROWS, ROWS), cols] = high
                    v_cat[half, s, pl.ds((3 * c + 1) * ROWS, ROWS), cols] = low
                    v_cat[half, s, pl.ds((3 * c + 2) * ROWS, ROWS), cols] = high

    def axial(ch, half, kh):
        for s in range(2):
            q_buf[s] = jnp.dot(axial_ref[kh], v_cat[half, s], preferred_element_type=f32)

        k = lax.broadcasted_iota(jnp.int32, (16, 256), 0)
        o = lax.broadcasted_iota(jnp.int32, (16, 256), 1) // 128
        scale = 1.0 / math.sqrt(NX * NZ)
        cos_of, sin_of = [], []
        for s in range(2):
            group = 2 * s + o
            steps = 4 * x_at + group if half == 0 else 4 * group + y_at
            psi = lax.rem(k * steps, 16).astype(f32) * (2.0 * math.pi / 16)
            cos_of.append(jnp.cos(psi) * scale)
            sin_of.append(jnp.sin(psi) * scale)
        lane = lax.broadcasted_iota(jnp.int32, (16, 128), 1)
        even = lane % 2 == 0
        mine = 8 * half + place[half] * 2 + core
        shift = lax.rem(128 - 8 * mine, 128)
        for blk in range(KX // 32):
            p = q = 0.0
            for s in range(2):
                a = q_buf[s, pl.ds(16 * blk, 16), :]
                b = q_buf[s, pl.ds(KX // 2 + 16 * blk, 16), :]
                p = p + (a * cos_of[s] - b * sin_of[s])
                q = q + (a * sin_of[s] + b * cos_of[s])
            p = p[:, :128] + p[:, 128:]
            q = q[:, :128] + q[:, 128:]
            q = jnp.where(even, -q, q)
            turn_buf[0, pl.ds(16 * blk, 16), :] = lane_roll(p, shift)
            turn_buf[1, pl.ds(16 * blk, 16), :] = lane_roll(q, shift)
        for blk in range(2):
            rows = pl.ds(128 * blk, 128)
            for which in range(2):
                flip_buf[which, blk] = turn_buf[which, rows, :].T
            for there in range(4):
                for ri in range(2):
                    straight = flip_buf[0, blk, pl.ds(2 * there + ri, 16, stride=8), :]
                    crossed = flip_buf[1, blk, pl.ds(2 * there + 1 - ri, 16, stride=8), :]
                    part_buf[ch, half, kh, there, ri, :, rows] = straight + crossed
        for step in (1, 3, 2):
            second_hop(ch, half, kh, step).start()

    def gather(ch, half, kh):
        total = part_buf[ch, half, kh, across[half]]
        for step in (1, 3, 2):
            second_hop(ch, half, kh, step, back=True).wait_recv()
        for step in range(1, 4):
            total = total + sum_buf[ch, half, kh, lax.rem(across[half] + step, 4)]
        out_ref[4, ch, half, kh] = total
        relay(ch, half, kh, 1)

    def body(q, _):
        @pl.when(q < groups // 2)
        def _():
            for s in range(2):
                load(s, q).wait()

        for odd in range(2):
            regroup(2 * q + odd - 2, (z_even, z_odd)[odd])
            if odd == 0:
                products(hi_odd, lo_odd, z_odd)
                residues(2 * q, hi_even, lo_even)
            else:
                products(hi_even, lo_even, z_even)
                residues(2 * q + 1, hi_odd, lo_odd)

        @pl.when(q == 1)
        def _():
            pl.semaphore_wait(barrier, 15)
            send_part(0, 0)

        for at, ch, part in ((3, 0, 1), (5, 0, 2), (6, 1, 0), (8, 1, 1)):

            @pl.when(q == at)
            def _():
                send_part(ch, part)

        return 0

    twist_in.wait()
    span_in.wait()
    lax.fori_loop(0, groups, body, 0)
    regroup(2 * groups - 2, z_even)
    products(hi_odd, lo_odd, z_odd)
    regroup(2 * groups - 1, z_odd)
    index = lax.broadcasted_iota(jnp.int32, (4 * BAND, 1), 0)
    own_plane = 2 * ring + index // BAND % 2
    gap = index % BAND
    code = jnp.where(index < 2 * BAND, own_plane, own_plane - gap) * BAND + gap
    lower = pair_ref[0:1, :]
    asked = lower * BAND + pair_ref[1:2, :] - lower == code
    asked = jnp.max(jnp.where(asked, 1.0, 0.0), axis=1, keepdims=True)
    asked = jnp.where((index >= 2 * BAND) & (own_plane < gap), 0.0, asked)
    flag_ref[...] = jnp.broadcast_to(asked, (4 * BAND, KX // 2))
    tables_in.wait()
    collect(0, 0)
    axial(0, 0, 0)
    collect(0, 1)
    axial(0, 1, 0)
    axial(0, 0, 1)
    axial(0, 1, 1)
    send_part(1, 2)
    for kh in range(2):
        for half in range(2):
            gather(0, half, kh)
    for kh in range(2):
        relays(0, kh, 2)
    collect(1, 0)
    axial(1, 0, 0)
    relays(0, 0, 3)
    collect(1, 1)
    axial(1, 1, 0)
    relays(0, 1, 3)
    axial(1, 0, 1)
    axial(1, 1, 1)
    relays(0, 0, 4)
    for half in range(2):
        gather(1, half, 0)
    relays(0, 1, 4)
    for half in range(2):
        gather(1, half, 1)
    def sent_by(ch):
        for half in range(2):
            for step, flip in first_order:
                first_hop(ch, half, step, flip).wait_send()
            for kh in range(2):
                for step in (1, 3, 2):
                    second_hop(ch, half, kh, step).wait_send()

    def relayed(ch):
        for half in range(2):
            for kh in range(2):
                for side in range(2):
                    hop(ch, half, kh, side, hops_of(ch, side)).wait_recv()
                    for s in range(1, hops_of(ch, side) + 1):
                        hop(ch, half, kh, side, s).wait_send()

    sent_by(0)
    for s in range(2, 5):
        for kh in range(2):
            relays(1, kh, s)
        if s == 2:
            sent_by(1)
        if s == 3:
            relayed(0)
    relayed(1)


def cross_kernel(flag_ref, spec_ref, band_ref, partner_ref):
    own = pl.program_id(0)
    half = pl.program_id(1)
    for i in range(2):

        @pl.when(own == i)
        def _():
            def pair(g, _):
                row = pl.multiple_of(g * 8, 8)
                for kh in range(2):
                    cols = pl.ds(KX // 2 * kh, KX // 2)
                    re0 = spec_ref[4, i, half, kh, 0, pl.ds(row, 8), :]
                    im0 = spec_ref[4, i, half, kh, 1, pl.ds(row, 8), :]
                    for which, out, sign in ((0, band_ref, 1), (1, partner_ref, -1)):
                        for d in range(BAND):
                            off, odd = divmod(i + sign * d, 2)
                            re1 = spec_ref[4 + off, odd, half, kh, 0, pl.ds(row, 8), :]
                            im1 = spec_ref[4 + off, odd, half, kh, 1, pl.ds(row, 8), :]
                            at = (2 * which + i) * BAND + d
                            ask = jnp.broadcast_to(flag_ref[at : at + 1, :], (8, KX // 2)) != 0.0
                            re, im = re0 * re1 + im0 * im1, im0 * re1 - re0 * im1
                            out[0, d, 0, pl.ds(row, 8), cols] = jnp.where(ask, re, 0.0)
                            out[0, d, 1, pl.ds(row, 8), cols] = jnp.where(ask, im, 0.0)
                return 0

            lax.fori_loop(0, 2, pair, 0)


def local(velocity, plane_slot, pair_list):
    span, twist, axial_cat = [jnp.asarray(t) for t in tables()]
    vmem = pl.BlockSpec(memory_space=pltpu.VMEM)
    hbm = pl.BlockSpec(memory_space=pltpu.HBM)
    slab = (2, 2, 2, 2, 16, KX // 2)
    dma = pltpu.SemaphoreType.DMA
    spectra, flags = pl.pallas_call(
        transform_kernel,
        out_shape=(
            jax.ShapeDtypeStruct((9,) + slab, f32),
            jax.ShapeDtypeStruct((4 * BAND, KX // 2), f32),
        ),
        in_specs=[pl.BlockSpec(memory_space=pltpu.SMEM), hbm, hbm, hbm, hbm, vmem],
        out_specs=(vmem, vmem),
        scratch_shapes=[
            pltpu.VMEM((2, ROWS, NZ), f32),
            pltpu.VMEM((512, 256), bf16),
            pltpu.VMEM((CLASSES, 2, 256), f32),
            pltpu.VMEM((2, KX, DEPTH), bf16),
            pltpu.VMEM((2, 8, 16, 512), bf16),
            pltpu.VMEM((2, 8, 16, 512), bf16),
            pltpu.VMEM((2, 8, 16, 512), bf16),
            pltpu.VMEM((2, 8, 16, 512), bf16),
            pltpu.VMEM((2, 8, 16, 128), f32),
            pltpu.VMEM((2, 8, 16, 128), f32),
            pltpu.VMEM((2, CLASSES, ROWS, 128), f32),
            pltpu.VMEM((2, 2, 8, ROWS, 128), f32),
            pltpu.VMEM((2, 2, DEPTH, 256), bf16),
            pltpu.VMEM((2, KX, 256), f32),
            pltpu.VMEM((2, KX // 2, 128), f32),
            pltpu.VMEM((2, 2, 128, 128), f32),
            pltpu.VMEM((2, 2, 2, 4, 2, 16, KX // 2), f32),
            pltpu.VMEM((2, 2, 2, 4, 2, 16, KX // 2), f32),
            dma((2, ROWS // 32)),
            dma((3,)),
            dma((2, 2)),
            dma((2, 2, 8)),
            dma((2, 2, 8)),
            dma((2, 2, 2, 4)),
            dma((2, 2, 2, 4)),
            dma((2, 2, 2, 2, 5)),
            dma((2, 2, 2, 2, 5)),
        ],
        compiler_params=pltpu.CompilerParams(
            collective_id=0, has_side_effects=True, vmem_limit_bytes=40 * 1024 * 1024
        ),
        name="transform",
    )(*[
        pltpu.with_memory_space_constraint(array, pltpu.HBM)
        for array in (plane_slot, velocity, span, twist, axial_cat, pair_list.T)
    ])

    share = KZ // PEERS
    out = jax.ShapeDtypeStruct((2, BAND, 2, share, KX), f32)
    block = pl.BlockSpec((1, BAND, 2, share // 2, KX), lambda i, h: (i, 0, 0, h, 0))
    band_cross, partner_cross = pl.pallas_call(
        cross_kernel,
        grid=(2, 2),
        out_shape=(out, out),
        in_specs=[vmem, vmem],
        out_specs=(block, block),
        compiler_params=pltpu.CompilerParams(vmem_limit_bytes=24 * 1024 * 1024),
        name="cross",
    )(flags, spectra)
    return (band_cross, partner_cross)


def solution(mesh):
    return jax.shard_map(
        local,
        mesh=mesh,
        in_specs=(P("plane", "pencil", None), P(), P()),
        out_specs=(P("plane", None, None, "pencil", None), P("plane", None, None, "pencil", None)),
        check_vma=False,
    )
```
